32 devices in a mesh: groups: 2 (over x), strip: 16 (over z, y, core).
Axes of the slice: x: 2, y: 2, z: 4, core: 2. Of those that a mesh axis runs over, the one named last changes fastest.
Arguments:
- queries: bfloat16 [32, 3, 128, 2240], P(('groups', 'strip')), parts along dimension 0, may hold values from -6 to 6
- keys: bfloat16 [32, 3, 128, 2240], P(('groups', 'strip')), parts along dimension 0, may hold values from -6 to 6
- values: bfloat16 [32, 3, 128, 2240], P(('groups', 'strip')), parts along dimension 0, may hold values from -6 to 6
- norm_gain: float32 [2240], replicated, may hold values from 0.1 to 1.9
- conv_weight: bfloat16 [3, 2240, 1152], P(None, None, 'strip'), may hold values from -0.078125 to 0.078125
Outputs:
- convolved: bfloat16 [32, 3, 128, 1152], P(('groups', 'strip')), parts along dimension 0
The draws below stay inside these ranges and needn't reach their ends.
There are 2 independent parts, one for each index of `groups`. The reference program is written for one: setup_inputs(seed, part) draws one part's arguments, and reference() takes and returns one part's arrays. A program takes and returns all parts, laid end to end along the dimension named above; an argument that names none is the same for every part. Nothing has to cross between parts.
All inputs are finite; a program needn't handle non-finite values.
Results may differ from the reference program's by a relative error of at most 0.0051.
Values may be sent and summed in bfloat16 or wider, within the bound.
No kernel may reach another device: no remote copies, remote signals or barrier semaphores. Data moves between devices by JAX's collectives and lax.ppermute only.
A program may use at most 128 MiB of HBM per device.

```python
import jax
import jax.numpy as jnp
from jax import lax

H = 20
DH = 112
D = 2240
C_OUT = 1152
TB = 4
FB = 3
P_SIZE = 128
SLOTS = 16
N_STRIP = 16


def block_levels(key, shape, shards, smallest, top_value):
    gain = 1.0
    for position, shards_of in shards:
        draws = jax.random.uniform(jax.random.fold_in(jax.random.fold_in(key, 6), position), (shards_of,), jnp.float32, smallest / len(shards), top_value / len(shards))
        gain = gain * jnp.repeat(jnp.exp(draws), shape[position] // shards_of).reshape((-1,) + (1,) * (len(shape) - 1 - position))
    return gain


def noise(rng, extent, width, most, split=(), kind=jnp.bfloat16):
    array = width * jax.random.normal(rng, extent, jnp.float32)
    if split:
        array = array * block_levels(rng, extent, split, -0.22, 0.18)
    return jnp.clip(array, -most, most).astype(kind)


def setup_inputs(seed: int = 0, part: int = 0) -> dict:
    splits = jax.random.split(jax.random.key(seed), 6)
    own_keys = jax.random.split(jax.random.fold_in(splits[5], part), 6)
    return {
        "queries": noise(own_keys[0], (SLOTS, FB, P_SIZE, D), 1.0, 6.0, ((0, 16),)),
        "keys": noise(own_keys[1], (SLOTS, FB, P_SIZE, D), 1.0, 6.0, ((0, 16),)),
        "values": noise(own_keys[2], (SLOTS, FB, P_SIZE, D), 1.0, 6.0, ((0, 16),)),
        "norm_gain": jnp.clip(1.0 + 0.18 * jax.random.normal(splits[3], (D,), jnp.float32), 0.1, 1.9),
        "conv_weight": noise(splits[4], (3, D, C_OUT), (3 * D) ** -0.5, 0.078125, ((2, 16),)),
    }


highest = lax.Precision.HIGHEST

def reference(queries, keys, values, norm_gain, conv_weight):
    strips = N_STRIP // TB
    per_block = strips * FB * P_SIZE
    key_blocks = jax.nn.relu(keys).reshape(TB, per_block, H, DH)
    value_blocks = values.reshape(TB, per_block, H, DH)

    def block_state(pair):
        key_part, value_part = pair
        key_float = key_part.astype(jnp.float32)
        state = jnp.einsum('nhd,nhe->hde', key_float, value_part.astype(jnp.float32), precision=highest)
        return (state, lax.optimization_barrier(jnp.sum(key_float, axis=0)))
    states, sums = lax.map(block_state, (key_blocks, value_blocks))
    states = jnp.cumsum(states, axis=0)
    sums = jnp.cumsum(sums, axis=0)
    rounded = states.astype(jnp.bfloat16)
    query_blocks = jax.nn.relu(queries).reshape(TB, per_block, H, DH)

    def block_output(triple):
        query_part, state_part, sum_part = triple
        query_float = query_part.astype(jnp.float32)
        numer = jnp.einsum('nhd,hde->nhe', query_float, state_part.astype(jnp.float32), precision=highest)
        denom = jnp.einsum('nhd,hd->nh', query_float, sum_part, precision=highest) + 1e-06
        attended = (numer / denom[..., None]).reshape(per_block, H * DH)
        scale = lax.rsqrt(lax.optimization_barrier(jnp.mean(attended * attended, axis=-1, keepdims=True)) + 1e-06)
        return (attended * scale * norm_gain).astype(jnp.bfloat16)
    normed = lax.map(block_output, (query_blocks, rounded, sums))
    frames = normed.reshape(TB, strips, FB, P_SIZE, H * DH).transpose(0, 2, 1, 3, 4).reshape(TB * FB, strips * P_SIZE, H * DH)
    padded = jnp.pad(frames, ((2, 0), (0, 0), (0, 0)))

    def frame_out(index):
        total = jnp.zeros((strips * P_SIZE, C_OUT), jnp.float32)
        for tap in range(3):
            piece = lax.dynamic_index_in_dim(padded, index + 2 - tap, 0, keepdims=False)
            total = total + jnp.dot(piece, conv_weight[tap], preferred_element_type=jnp.float32)
        return total.astype(jnp.bfloat16)
    outputs = lax.map(frame_out, jnp.arange(TB * FB, dtype=jnp.int32))
    outputs = outputs.reshape(TB, FB, strips, P_SIZE, C_OUT).transpose(0, 2, 1, 3, 4)
    return outputs.reshape(N_STRIP, FB, P_SIZE, C_OUT)
```

```python
import functools

import jax
import jax.numpy as jnp
from jax import lax
from jax.experimental import pallas as pl
from jax.experimental.pallas import tpu as pltpu
from jax.sharding import PartitionSpec as P


H = 20
DH = 112
TB = 4
EPS = 1e-06
LANES = 128
ANY = pl.BlockSpec(memory_space=pl.ANY)
VMEM = pl.BlockSpec(memory_space=pltpu.VMEM)
SMEM = pl.BlockSpec(memory_space=pltpu.SMEM)


def from_behind(block, axis, distance):
    devices = range(lax.axis_size(axis))
    route = [(i - distance, i) for i in devices if i - distance in devices]
    return lax.ppermute(block, axis, route)


def generic(queries, keys, values, norm_gain, conv_weight):
    _, frames, pixels, width = queries.shape
    devices = lax.axis_size("strip")
    strips = devices // TB
    block_index = lax.axis_index("strip") // strips
    count = frames * pixels
    key_heads = jax.nn.relu(keys).reshape(count, H, DH)
    value_heads = values.reshape(count, H, DH)
    key_value = jnp.einsum(
        "nhd,nhe->hde", key_heads, value_heads, preferred_element_type=jnp.float32
    )
    key_sums = jnp.sum(key_heads, axis=0, dtype=jnp.float32)
    state_len = H * DH * DH
    raw_len = state_len + width
    row_len = (raw_len + devices - 1) // devices * devices
    row = jnp.concatenate(
        [key_value.reshape(-1), key_sums.reshape(-1), jnp.zeros((row_len - raw_len,), jnp.float32)]
    )
    later_blocks = (jnp.arange(TB) >= block_index).astype(jnp.float32)[:, None]
    share = lax.psum_scatter(later_blocks * row[None, :], "strip", scatter_dimension=1, tiled=True)
    outgoing = jnp.broadcast_to(share[:, None, :], (TB, strips, share.shape[1])).reshape(
        devices, share.shape[1]
    )
    returned = lax.all_to_all(outgoing, "strip", split_axis=0, concat_axis=1, tiled=True).reshape(
        -1
    )
    state = returned[:state_len].reshape(H, DH, DH)
    summed = returned[state_len:raw_len].reshape(H, DH)
    state_rounded = state.astype(jnp.bfloat16)
    query_heads = jax.nn.relu(queries).reshape(count, H, DH)
    numer = jnp.einsum(
        "nhd,hde->nhe", query_heads, state_rounded, preferred_element_type=jnp.float32
    )
    denom = (
        jnp.einsum(
            "nhd,hd->nh", query_heads.astype(jnp.float32), summed, precision=lax.Precision.HIGHEST
        )
        + EPS
    )
    attended = (numer / denom[..., None]).reshape(count, width)
    scale = lax.rsqrt(jnp.mean(attended * attended, axis=-1, keepdims=True) + EPS)
    normed = (attended * scale * norm_gain).astype(jnp.bfloat16).reshape(frames, pixels, width)
    rim = from_behind(normed[-2:], "strip", strips)
    extended = jnp.concatenate([rim, normed], axis=0)
    stacked = jnp.concatenate([normed, extended[1:-1], extended[:-2]], axis=-1).reshape(
        -1, 3 * width
    )
    full_taps = lax.all_gather(conv_weight, "strip", axis=2, tiled=True)
    mixed = jnp.dot(
        stacked, full_taps.reshape(3 * width, -1), preferred_element_type=jnp.float32
    ).astype(jnp.bfloat16)
    return mixed.reshape(1, frames, pixels, mixed.shape[-1])


def vm(value):
    return pltpu.with_memory_space_constraint(value, pltpu.VMEM)


def limit(mib):
    return pltpu.CompilerParams(vmem_limit_bytes=mib * 2**20)


def slice_kernel(step, x_ref, from_ref, to_ref, sem):
    at = pl.ds(pl.multiple_of(x_ref[0] * step, 8), to_ref.shape[0])
    copy = pltpu.make_async_copy(from_ref.at[at, :], to_ref, sem)
    copy.start()
    copy.wait()


def half_of(x, whole, half):
    rows, width = whole.shape
    return pl.pallas_call(
        functools.partial(slice_kernel, rows - half),
        in_specs=[SMEM, ANY],
        out_specs=VMEM,
        out_shape=pltpu.VMEM((half, width), whole.dtype),
        scratch_shapes=[pltpu.SemaphoreType.DMA],
        compiler_params=limit(4),
        name="half_of",
    )(x, whole)


def state_kernel(mine, k_ref, v_ref, *outs):
    step = pl.program_id(0)
    frames, rows, pixels = k_ref.shape
    heads = rows // DH
    fill = (lax.broadcasted_iota(jnp.int32, (LANES - DH, frames * pixels), 0) == 0).astype(
        jnp.bfloat16
    )

    for head in range(heads):
        part = pl.ds(head * DH, DH)
        k = jnp.concatenate([k_ref[f, part, :] for f in range(frames)], axis=1)
        v = jnp.concatenate([v_ref[f, part, :] for f in range(frames)], axis=1)
        k = jnp.maximum(k, jnp.zeros_like(k))
        v = jnp.concatenate([v, fill], axis=0)
        both = lax.dot_general(
            k, v, (((1,), (1,)), ((), ())), preferred_element_type=jnp.float32
        ).astype(jnp.bfloat16)
        for i, out in enumerate(outs):

            @pl.when(step % 2 == i)
            def _(out=out):
                out[part, :] = both


def local_state(mine, keys, values):
    frames, width, pixels = keys.shape
    quarter = width // 4
    spec = pl.BlockSpec((frames, quarter, pixels), lambda r, m: (0, r ^ m[0], 0))
    return pl.pallas_call(
        state_kernel,
        grid_spec=pltpu.PrefetchScalarGridSpec(
            num_scalar_prefetch=1,
            grid=(4,),
            in_specs=[spec, spec],
            out_specs=[pl.BlockSpec((quarter, LANES), lambda r, m: (r // 2, 0))] * 2,
        ),
        out_shape=[jax.ShapeDtypeStruct((2 * quarter, LANES), jnp.bfloat16)] * 2,
        name="local_state",
    )(mine, keys, values)


def add_up(*parts):
    total = parts[0].astype(jnp.float32)
    for part in parts[1:]:
        total = total + part.astype(jnp.float32)
    return total.astype(parts[0].dtype)


def attend_kernel(chosen, mine, q_ref, s0, s1, s2, s3, gain_ref, out_ref, attended):
    heads = s0.shape[0] // DH
    lanes = out_ref.shape[1]
    squares = jnp.zeros((8, lanes), jnp.float32)
    for r, state_ref in enumerate((s0, s1, s2, s3)):
        first = (r ^ mine[0]) * heads
        for i in range(heads):
            at = pl.ds(pl.multiple_of((first + i) * DH, 16), DH)
            q = jnp.concatenate([q_ref[f, at, :] for f in chosen], axis=1)
            q = jnp.maximum(q, jnp.zeros_like(q))
            s = state_ref[pl.ds(i * DH, DH), :]
            both = lax.dot_general(
                s, q, (((0,), (0,)), ((), ())), preferred_element_type=jnp.float32
            )
            a = both[:DH] * (1.0 / (both[DH : DH + 1] + EPS))
            attended[at, :] = a
            squares = squares + jnp.sum((a * a).reshape(DH // 8, 8, lanes), axis=0)
    width = attended.shape[0]
    mean = jnp.sum(squares, axis=0, keepdims=True) / width
    scale = lax.rsqrt(mean + EPS)
    for i in range(width // DH):
        at = pl.ds(i * DH, DH)
        gain = gain_ref[at, :]
        gain = jnp.concatenate([gain] * (lanes // LANES), axis=1)
        out_ref[at, :] = (attended[at, :] * scale * gain).astype(out_ref.dtype)


def attend(chosen, mine, queries, states, gain):
    _, width, pixels = queries.shape
    lanes = len(chosen) * pixels
    return pl.pallas_call(
        functools.partial(attend_kernel, chosen),
        in_specs=[SMEM] + [VMEM] * 6,
        out_specs=VMEM,
        out_shape=pltpu.VMEM((width, lanes), jnp.bfloat16),
        scratch_shapes=[pltpu.VMEM((width, lanes), jnp.float32)],
        compiler_params=limit(16),
        name="attend",
    )(mine, queries, *states, gain)


def place(x, cols, half, taps, shards, refs, w, sems):
    rows = 3 * cols

    def plan(own_top):
        copies = {t: [] for t in taps}
        count = 0
        spans = []
        for kind, block, *which in shards:
            if kind == "whole":
                spans.append((refs[which[0]], block, 0, rows, 0))
            else:
                for ref, top in ((refs[which[0]], own_top), (refs[which[1]], not own_top)):
                    if top:
                        spans.append((ref, block, 0, half, 0))
                    else:
                        spans.append((ref, block, half, rows, rows - half))
        for t in taps:
            for ref, block, lo, hi, shift in spans:
                a, b = max(lo, t * cols), min(hi, (t + 1) * cols)
                if a < b:
                    at = pl.ds(pl.multiple_of(block * cols + a - t * cols, 8), b - a)
                    copies[t].append(
                        pltpu.make_async_copy(
                            ref.at[pl.ds(a - shift, b - a), :], w.at[t, at, :], sems.at[count]
                        )
                    )
                    count += 1
        return copies

    def each(do, only):
        for flag in (True, False):

            @pl.when((x == 0) == flag)
            def _(flag=flag):
                copies = plan(flag)
                for t in only:
                    for c in copies[t]:
                        do(c)

    each(lambda c: c.start(), taps)
    return lambda t: each(lambda c: c.wait(), (t,))


def dot(a, b):
    return lax.dot_general(a, b, (((1,), (0,)), ((), ())), preferred_element_type=jnp.float32)


def where_of(code):
    return code // (4 * TB), code // 4 % TB, code // 2 % 2, code % 2


def shards_of(late, z, y):
    if not late:
        here, beside = z % 2, 1 - z % 2
        return [
            ("halves", beside * 2 + y, 3, 4),
            ("halves", beside * 2 + 1 - y, 5, 6),
            ("whole", here * 2 + y, 0),
            ("halves", here * 2 + 1 - y, 1, 2),
        ]
    first = jnp.where(z < TB // 2, 0, 1)
    return [
        ("halves", first * 2 + y, 0, 1),
        ("halves", first * 2 + 1 - y, 2, 3),
        ("halves", (1 - first) * 2 + y, 4, 5),
        ("halves", (1 - first) * 2 + 1 - y, 6, 7),
    ]


def both_cores(own, other, at):
    return jnp.concatenate([own[:, at], other[:, at]], axis=1)


def rim_kernel(cols, half, late, code, n_own, n_other, *refs):
    pieces = refs[:-4]
    keep, give, w, sems = refs[-4:]
    x, z, y, _ = where_of(code[0])
    wait = place(x, cols, half, (2, 1, 0), shards_of(late, z, y), pieces, w, sems)
    p = n_own.shape[1] // 2
    first = both_cores(n_own, n_other, pl.ds(0, p))
    last = both_cores(n_own, n_other, pl.ds(p, p))
    wait(2)
    w2 = w[2]
    two = dot(w2, last).astype(keep.dtype)
    keep[:, p:], give[:, p:] = two[:, :p], two[:, p:]
    one = dot(w2, first)
    wait(1)
    one = (one + dot(w[1], last)).astype(keep.dtype)
    keep[:, :p], give[:, :p] = one[:, :p], one[:, p:]
    wait(0)


def own_kernel(n_own, n_other, z_own, z_other, w, keep, give):
    p = n_own.shape[1] // 2
    zero = jnp.concatenate([z_own[...], z_other[...]], axis=1)
    first = both_cores(n_own, n_other, pl.ds(0, p))
    last = both_cores(n_own, n_other, pl.ds(p, p))
    totals = (
        dot(w[0], zero),
        dot(w[0], first) + dot(w[1], zero),
        dot(w[0], last) + dot(w[1], first) + dot(w[2], zero),
    )
    for f, total in enumerate(totals):
        at = pl.ds(f * p, p)
        keep[:, at], give[:, at] = total[:, :p], total[:, p:]


def out_kernel(cols, code, *refs):
    sums, rims, (out, rows) = refs[:4], refs[4:8], refs[8:]
    p = out.shape[1]
    _, z, _, core = where_of(code[0])
    odd = z % 2 == 1
    for f in range(3):
        for late in range(2):
            pair = z // 2 if late == 0 else 1 - z // 2
            for who in range(2):
                total = sums[2 * late + who][:, pl.ds(f * p, p)]
                if f < 2:
                    at = pl.ds(f * p, p)
                    same, flipped = rims[2 * late + who], rims[2 * (1 - late) + who]
                    rim = jnp.where(odd, same[:, at], flipped[:, at])
                    total = total + rim.astype(jnp.float32)
                c = core if who == 0 else 1 - core
                blocks = total.shape[0] // cols
                for i in range(blocks):
                    to = ((pair * blocks + i) * 2 + c) * cols
                    rows[pl.ds(pl.multiple_of(to, 8), cols), :] = total[i * cols : (i + 1) * cols]
        for j in range(rows.shape[0] // LANES):
            tile = rows[pl.ds(j * LANES, LANES), :]
            out[f, :, pl.ds(j * LANES, LANES)] = tile.T.astype(out.dtype)


def tuned(queries, keys, values, norm_gain, conv_weight):
    _, frames, pixels, width = queries.shape
    cols = conv_weight.shape[2]
    axes = ("groups", "strip")
    groups, devices = lax.axis_size("groups"), lax.axis_size("strip")
    strips = devices // TB
    x, s = lax.axis_index("groups"), lax.axis_index("strip")
    z, inside = s // strips, s % strips
    y, core = inside // 2, inside % 2

    def send(block, where):
        route = []
        for g in range(groups):
            for d in range(devices):
                to = where(g, d)
                if to is not None:
                    route.append((g * devices + d, to[0] * devices + to[1]))
        return lax.ppermute(block, axes, route)

    def to_core(g, d):
        return g, d ^ 1

    def to_y(g, d):
        return g, d ^ 2

    def to_x(g, d):
        return 1 - g, d

    def up(r):
        return lambda g, d: (g, d + r * strips) if d + r * strips < devices else None

    def up_across(g, d):
        return (g, (d + strips) ^ 1) if d + strips < devices else None

    def along(**pairs):
        table = {int(a[1:]): b for a, b in pairs.items()}
        return lambda g, d: (
            (g, table[d // strips] * strips + d % strips) if d // strips in table else None
        )

    mine = inside.astype(jnp.int32).reshape(1)
    side = x.astype(jnp.int32).reshape(1)
    code = (x * devices // strips * 4 + z * 4 + y * 2 + core).astype(jnp.int32).reshape(1)
    k = keys[0].transpose(0, 2, 1)
    v = values[0].transpose(0, 2, 1)
    q = queries[0].transpose(0, 2, 1)
    q = vm(q)
    gain = vm(jnp.broadcast_to(norm_gain[:, None], (width, LANES)))

    rows = 3 * cols
    half = -(-rows // 16) * 8
    whole = conv_weight.transpose(0, 2, 1).reshape(rows, width)
    piece = half_of(side, whole, half)
    zp1 = send(piece, along(z0=1, z1=0, z2=3, z3=2))
    zp2 = send(piece, along(z1=2, z2=1))
    zp3 = send(zp1, along(z1=2, z2=1))
    zp4 = send(zp2, along(z1=0, z2=3))
    zp5 = send(zp3, along(z1=0, z2=3))
    outer = (z == 0) | (z == TB - 1)
    slot_b = jnp.where(outer, zp4, zp2)
    slot_c = jnp.where(outer, zp5, zp3)
    y0 = send(piece, to_y)
    ya = send(zp1, to_y)
    yb = send(slot_b, to_y)
    yc = send(slot_c, to_y)
    rest = half_of(1 - side, whole, half)
    early_pieces = [whole, y0, send(rest, to_y), zp1, send(zp1, to_x), ya, send(ya, to_x)]
    late_pieces = [
        slot_b,
        send(slot_b, to_x),
        yb,
        send(yb, to_x),
        slot_c,
        send(slot_c, to_x),
        yc,
        send(yc, to_x),
    ]

    quarter = width // 4
    kept, given = local_state(mine, k, v)
    chip = add_up(kept, send(given, to_core))
    plane = add_up(chip[:quarter], send(chip[quarter:], to_y))
    share = add_up(plane, *[send(plane, up(r)) for r in (1, 2, 3)])
    beside = send(share, to_y)
    states = [share, send(share, to_core), beside, send(beside, to_core)]
    states = [vm(s) for s in states]

    late = attend((1, 2), mine, q, states, gain)
    late_other = vm(send(late, to_core))
    early = attend((0,), mine, q, states, gain)
    early_other = vm(send(early, to_core))

    part_rows = cols * devices // 4
    sums, rims = [], []
    for name, pieces in (("a", early_pieces), ("b", late_pieces)):
        keep, give, taps = pl.pallas_call(
            functools.partial(rim_kernel, cols, half, name == "b"),
            in_specs=[SMEM] + [VMEM] * (2 + len(pieces)),
            out_specs=[VMEM] * 3,
            out_shape=[pltpu.VMEM((part_rows, 2 * pixels), jnp.bfloat16)] * 2
            + [pltpu.VMEM((3, part_rows, width), jnp.bfloat16)],
            scratch_shapes=[pltpu.SemaphoreType.DMA((24,))],
            compiler_params=limit(16),
            name="rim",
        )(code, late, late_other, *[vm(piece) for piece in pieces])
        rims += [send(keep, up(1)), send(give, up_across)]
        keep, give = pl.pallas_call(
            own_kernel,
            in_specs=[VMEM] * 5,
            out_specs=[VMEM] * 2,
            out_shape=[pltpu.VMEM((part_rows, 3 * pixels), jnp.float32)] * 2,
            compiler_params=limit(16),
            name="own",
        )(late, late_other, early, early_other, taps)
        sums += [keep, send(give, to_core)]

    result = pl.pallas_call(
        functools.partial(out_kernel, cols),
        in_specs=[SMEM] + [VMEM] * 8,
        out_specs=VMEM,
        out_shape=jax.ShapeDtypeStruct((frames, pixels, 4 * part_rows), jnp.bfloat16),
        scratch_shapes=[pltpu.VMEM((4 * part_rows, pixels), jnp.float32)],
        compiler_params=limit(16),
        name="out",
    )(code, *[vm(part) for part in sums + rims])
    return result[None]


def solution(mesh):
    placed = (
        P(("groups", "strip"), None, None, None),
        P(("groups", "strip"), None, None, None),
        P(("groups", "strip"), None, None, None),
        P(),
        P(None, None, "strip"),
    )

    groups, devices = mesh.shape["groups"], mesh.shape["strip"]
    square = groups == 2 and devices == 4 * TB

    def per_device(queries, keys, values, norm_gain, conv_weight):
        _, frames, pixels, width = queries.shape
        cols = conv_weight.shape[2]
        fits = (
            square
            and frames == 3
            and pixels == LANES
            and width == H * DH
            and cols % 8 == 0
            and cols * devices % LANES == 0
        )
        form = tuned if fits else generic
        return form(queries, keys, values, norm_gain, conv_weight)

    return jax.shard_map(
        per_device,
        mesh=mesh,
        in_specs=placed,
        out_specs=P(("groups", "strip"), None, None, None),
        check_vma=False,
    )
```

```python
import functools

import jax
import jax.numpy as jnp
from jax import lax
from jax.experimental import pallas as pl
from jax.experimental.pallas import tpu as pltpu
from jax.sharding import PartitionSpec as P


H = 20
DH = 112
TB = 4
EPS = 1e-06
LANES = 128
ANY = pl.BlockSpec(memory_space=pl.ANY)
VMEM = pl.BlockSpec(memory_space=pltpu.VMEM)
SMEM = pl.BlockSpec(memory_space=pltpu.SMEM)


def from_behind(block, axis, distance):
    devices = range(lax.axis_size(axis))
    route = [(i - distance, i) for i in devices if i - distance in devices]
    return lax.ppermute(block, axis, route)


def generic(queries, keys, values, norm_gain, conv_weight):
    _, frames, pixels, width = queries.shape
    devices = lax.axis_size("strip")
    strips = devices // TB
    block_index = lax.axis_index("strip") // strips
    count = frames * pixels
    key_heads = jax.nn.relu(keys).reshape(count, H, DH)
    value_heads = values.reshape(count, H, DH)
    key_value = jnp.einsum(
        "nhd,nhe->hde", key_heads, value_heads, preferred_element_type=jnp.float32
    )
    key_sums = jnp.sum(key_heads, axis=0, dtype=jnp.float32)
    state_len = H * DH * DH
    raw_len = state_len + width
    row_len = (raw_len + devices - 1) // devices * devices
    row = jnp.concatenate(
        [key_value.reshape(-1), key_sums.reshape(-1), jnp.zeros((row_len - raw_len,), jnp.float32)]
    )
    later_blocks = (jnp.arange(TB) >= block_index).astype(jnp.float32)[:, None]
    share = lax.psum_scatter(later_blocks * row[None, :], "strip", scatter_dimension=1, tiled=True)
    outgoing = jnp.broadcast_to(share[:, None, :], (TB, strips, share.shape[1])).reshape(
        devices, share.shape[1]
    )
    returned = lax.all_to_all(outgoing, "strip", split_axis=0, concat_axis=1, tiled=True).reshape(
        -1
    )
    state = returned[:state_len].reshape(H, DH, DH)
    summed = returned[state_len:raw_len].reshape(H, DH)
    state_rounded = state.astype(jnp.bfloat16)
    query_heads = jax.nn.relu(queries).reshape(count, H, DH)
    numer = jnp.einsum(
        "nhd,hde->nhe", query_heads, state_rounded, preferred_element_type=jnp.float32
    )
    denom = (
        jnp.einsum(
            "nhd,hd->nh", query_heads.astype(jnp.float32), summed, precision=lax.Precision.HIGHEST
        )
        + EPS
    )
    attended = (numer / denom[..., None]).reshape(count, width)
    scale = lax.rsqrt(jnp.mean(attended * attended, axis=-1, keepdims=True) + EPS)
    normed = (attended * scale * norm_gain).astype(jnp.bfloat16).reshape(frames, pixels, width)
    rim = from_behind(normed[-2:], "strip", strips)
    extended = jnp.concatenate([rim, normed], axis=0)
    stacked = jnp.concatenate([normed, extended[1:-1], extended[:-2]], axis=-1).reshape(
        -1, 3 * width
    )
    full_taps = lax.all_gather(conv_weight, "strip", axis=2, tiled=True)
    mixed = jnp.dot(
        stacked, full_taps.reshape(3 * width, -1), preferred_element_type=jnp.float32
    ).astype(jnp.bfloat16)
    return mixed.reshape(1, frames, pixels, mixed.shape[-1])


def vm(value):
    return pltpu.with_memory_space_constraint(value, pltpu.VMEM)


def hbm(value):
    return pltpu.with_memory_space_constraint(value, pltpu.HBM)


def limit(mib):
    return pltpu.CompilerParams(vmem_limit_bytes=mib * 2**20)


def slice_kernel(step, x_ref, from_ref, to_ref, sems):
    count = to_ref.shape[0] // sems.shape[0]
    copies = []
    for i in range(sems.shape[0]):
        at = pl.ds(pl.multiple_of(x_ref[0] * step + i * count, 8), count)
        copies.append(
            pltpu.make_async_copy(
                from_ref.at[at, :], to_ref.at[pl.ds(i * count, count), :], sems.at[i]
            )
        )
    for copy in copies:
        copy.start()
    for copy in copies:
        copy.wait()


def half_of(x, whole, half):
    rows, width = whole.shape
    return pl.pallas_call(
        functools.partial(slice_kernel, rows - half),
        in_specs=[SMEM, ANY],
        out_specs=VMEM,
        out_shape=pltpu.VMEM((half, width), whole.dtype),
        scratch_shapes=[pltpu.SemaphoreType.DMA((half // 8,))],
        compiler_params=limit(4),
        name="half_of",
    )(x, hbm(whole))


def state_kernel(mine, k_ref, v_ref, *outs):
    step = pl.program_id(0)
    frames, rows, pixels = k_ref.shape
    heads = rows // DH
    fill = (lax.broadcasted_iota(jnp.int32, (LANES - DH, frames * pixels), 0) == 0).astype(
        jnp.bfloat16
    )

    for head in range(heads):
        part = pl.ds(head * DH, DH)
        k = jnp.concatenate([k_ref[f, part, :] for f in range(frames)], axis=1)
        v = jnp.concatenate([v_ref[f, part, :] for f in range(frames)], axis=1)
        k = jnp.maximum(k, jnp.zeros_like(k))
        v = jnp.concatenate([v, fill], axis=0)
        both = lax.dot_general(
            k, v, (((1,), (1,)), ((), ())), preferred_element_type=jnp.float32
        ).astype(jnp.bfloat16)
        for i, out in enumerate(outs):

            @pl.when(step % 2 == i)
            def _(out=out):
                out[part, :] = both


def local_state(mine, keys, values):
    frames, width, pixels = keys.shape
    quarter = width // 4
    spec = pl.BlockSpec((frames, quarter, pixels), lambda r, m: (0, r ^ m[0], 0))
    return pl.pallas_call(
        state_kernel,
        grid_spec=pltpu.PrefetchScalarGridSpec(
            num_scalar_prefetch=1,
            grid=(4,),
            in_specs=[spec, spec],
            out_specs=[pl.BlockSpec((quarter, LANES), lambda r, m: (r // 2, 0))] * 2,
        ),
        out_shape=[jax.ShapeDtypeStruct((2 * quarter, LANES), jnp.bfloat16)] * 2,
        name="local_state",
    )(mine, keys, values)


def add_up(*parts):
    total = parts[0].astype(jnp.float32)
    for part in parts[1:]:
        total = total + part.astype(jnp.float32)
    return total.astype(parts[0].dtype)


def attend_kernel(chosen, mine, q_ref, s0, s1, s2, s3, gain_ref, out_ref, attended):
    heads = s0.shape[0] // DH
    lanes = out_ref.shape[1]
    squares = jnp.zeros((8, lanes), jnp.float32)
    for r, state_ref in enumerate((s0, s1, s2, s3)):
        first = (r ^ mine[0]) * heads
        for i in range(heads):
            at = pl.ds(pl.multiple_of((first + i) * DH, 16), DH)
            q = jnp.concatenate([q_ref[f, at, :] for f in chosen], axis=1)
            q = jnp.maximum(q, jnp.zeros_like(q))
            s = state_ref[pl.ds(i * DH, DH), :]
            both = lax.dot_general(
                s, q, (((0,), (0,)), ((), ())), preferred_element_type=jnp.float32
            )
            a = both[:DH] * (1.0 / (both[DH : DH + 1] + EPS))
            attended[at, :] = a
            squares = squares + jnp.sum((a * a).reshape(DH // 8, 8, lanes), axis=0)
    width = attended.shape[0]
    mean = jnp.sum(squares, axis=0, keepdims=True) / width
    scale = lax.rsqrt(mean + EPS)
    for i in range(width // DH):
        at = pl.ds(i * DH, DH)
        gain = gain_ref[at, :]
        gain = jnp.concatenate([gain] * (lanes // LANES), axis=1)
        out_ref[at, :] = (attended[at, :] * scale * gain).astype(out_ref.dtype)


def attend(chosen, mine, queries, states, gain):
    _, width, pixels = queries.shape
    lanes = len(chosen) * pixels
    return pl.pallas_call(
        functools.partial(attend_kernel, chosen),
        in_specs=[SMEM] + [VMEM] * 6,
        out_specs=VMEM,
        out_shape=pltpu.VMEM((width, lanes), jnp.bfloat16),
        scratch_shapes=[pltpu.VMEM((width, lanes), jnp.float32)],
        compiler_params=limit(16),
        name="attend",
    )(mine, queries, *states, gain)


def place(x, outer, cols, half, tap, shards, refs, w):
    rows = 3 * cols
    lo_tap, hi_tap = tap * cols, (tap + 1) * cols

    def put(ref, block, lo, hi, shift):
        a, b = max(lo, lo_tap), min(hi, hi_tap)
        if a < b:
            at = pl.ds(pl.multiple_of(block * cols + a - lo_tap, 8), b - a)
            part = pl.ds(a - shift, b - a)
            if isinstance(ref, tuple):
                w[at, :] = jnp.where(outer, ref[0][part, :], ref[1][part, :])
            else:
                w[at, :] = ref[part, :]

    for kind, block, *which in shards:
        if kind == "whole":
            put(refs[which[0]], block, 0, rows, 0)

    for flag in (True, False):

        @pl.when((x == 0) == flag)
        def _(flag=flag):
            for kind, block, *which in shards:
                if kind == "halves":
                    for ref, top in ((refs[which[0]], flag), (refs[which[1]], not flag)):
                        if top:
                            put(ref, block, 0, half, 0)
                        else:
                            put(ref, block, half, rows, rows - half)


def dot(a, b):
    return lax.dot_general(a, b, (((1,), (0,)), ((), ())), preferred_element_type=jnp.float32)


def where_of(code):
    return code // (4 * TB), code // 4 % TB, code // 2 % 2, code % 2


def first_late(z):
    return jnp.where(z < TB // 2, 0, 1)


def shards_of(part, z, y):
    if part == 0:
        here, beside = z % 2, 1 - z % 2
        return [
            ("halves", beside * 2 + y, 3, 4),
            ("halves", beside * 2 + 1 - y, 5, 6),
            ("whole", here * 2 + y, 0),
            ("halves", here * 2 + 1 - y, 1, 2),
        ]
    return [("halves", y, 0, 1), ("halves", 1 - y, 2, 3)]


def both_cores(own, other, at):
    return jnp.concatenate([own[:, at], other[:, at]], axis=1)


def rim_kernel(cols, half, part, code, n_own, n_other, *refs):
    pieces, (out, w) = list(refs[:-2]), refs[-2:]
    x, z, y, _ = where_of(code[0])
    outer = (z == 0) | (z == TB - 1)
    if part == 1:
        pieces[1:3] = [(pieces[1], pieces[2])]
    for tap in (2, 1, 0):
        place(x, outer, cols, half, tap, shards_of(part, z, y), pieces, w.at[tap])
    p = n_own.shape[1] // 2
    first = both_cores(n_own, n_other, pl.ds(0, p))
    last = both_cores(n_own, n_other, pl.ds(p, p))
    out[:, 2 * p :] = dot(w[2], last).astype(out.dtype)
    out[:, : 2 * p] = (dot(w[2], first) + dot(w[1], last)).astype(out.dtype)


def own_kernel(late, code, n_own, n_other, z_own, z_other, *refs):
    taps, (keep, give) = refs[:-2], refs[-2:]
    _, z, _, _ = where_of(code[0])
    p = n_own.shape[1] // 2
    zero = jnp.concatenate([z_own[...], z_other[...]], axis=1)
    first = both_cores(n_own, n_other, pl.ds(0, p))
    last = both_cores(n_own, n_other, pl.ds(p, p))
    for i, w in enumerate(taps):
        count = w.shape[1]
        to = i * count
        if late:
            nearer = first_late(z)
            to = (nearer if i == 0 else 1 - nearer) * count
        rows = pl.ds(pl.multiple_of(to, 8), count)
        totals = (
            dot(w[0], zero),
            dot(w[0], first) + dot(w[1], zero),
            dot(w[0], last) + dot(w[1], first) + dot(w[2], zero),
        )
        for f, total in enumerate(totals):
            at = pl.ds(f * p, p)
            keep[rows, at], give[rows, at] = total[:, :p], total[:, p:]


def out_kernel(cols, code, *refs):
    sums, rims, (out, rows) = refs[:4], refs[4:10], refs[10:]
    p = out.shape[1]
    _, z, _, core = where_of(code[0])
    behind = z - 1
    behind_pair = behind // 2
    nearer = first_late(behind)
    count = 2 * cols
    for f in range(3):
        for late in range(2):
            pair = z // 2 if late == 0 else 1 - z // 2
            for j in range(2):
                for who in range(2):
                    total = sums[2 * late + who][pl.ds(j * count, count), pl.ds(f * p, p)]
                    if f < 2:
                        at = pl.ds((2 * f + who) * p, p)
                        near, mid, far = rims[who], rims[2 + who], rims[4 + who]
                        rim = jnp.where(
                            pair == behind_pair,
                            near[pl.ds(j * count, count), at],
                            jnp.where(nearer == j, mid[:, at], far[:, at]),
                        )
                        total = total + rim.astype(jnp.float32)
                    c = core if who == 0 else 1 - core
                    for i in range(2):
                        to = (((pair * 2 + j) * 2 + i) * 2 + c) * cols
                        rows[pl.ds(pl.multiple_of(to, 8), cols), :] = total[
                            i * cols : (i + 1) * cols
                        ]
        for j in range(rows.shape[0] // LANES):
            tile = rows[pl.ds(j * LANES, LANES), :]
            out[f, :, pl.ds(j * LANES, LANES)] = tile.T.astype(out.dtype)


def tuned(queries, keys, values, norm_gain, conv_weight):
    _, frames, pixels, width = queries.shape
    cols = conv_weight.shape[2]
    axes = ("groups", "strip")
    groups, devices = lax.axis_size("groups"), lax.axis_size("strip")
    strips = devices // TB
    x, s = lax.axis_index("groups"), lax.axis_index("strip")
    z, inside = s // strips, s % strips
    y, core = inside // 2, inside % 2

    def send(block, where):
        route = []
        for g in range(groups):
            for d in range(devices):
                to = where(g, d)
                if to is not None:
                    route.append((g * devices + d, to[0] * devices + to[1]))
        return lax.ppermute(block, axes, route)

    def to_core(g, d):
        return g, d ^ 1

    def to_y(g, d):
        return g, d ^ 2

    def to_x(g, d):
        return 1 - g, d

    def up(r):
        return lambda g, d: (g, d + r * strips) if d + r * strips < devices else None

    def along(**pairs):
        table = {int(a[1:]): b for a, b in pairs.items()}
        return lambda g, d: (
            (g, table[d // strips] * strips + d % strips) if d // strips in table else None
        )

    mine = inside.astype(jnp.int32).reshape(1)
    side = x.astype(jnp.int32).reshape(1)
    code = (x * devices // strips * 4 + z * 4 + y * 2 + core).astype(jnp.int32).reshape(1)
    k = keys[0].transpose(0, 2, 1)
    v = values[0].transpose(0, 2, 1)
    q = queries[0].transpose(0, 2, 1)
    q = vm(q)
    gain = vm(jnp.broadcast_to(norm_gain[:, None], (width, LANES)))

    rows = 3 * cols
    half = -(-rows // 16) * 8
    whole = conv_weight.transpose(0, 2, 1).reshape(rows, width)
    piece = half_of(side, whole, half)
    rest = half_of(1 - side, whole, half)
    zp1 = send(piece, along(z0=1, z1=0, z2=3, z3=2))
    zp2 = send(piece, along(z1=2, z2=1))
    zp3 = send(zp1, along(z1=2, z2=1))
    zp4 = send(zp2, along(z1=0, z2=3))
    zp5 = send(zp3, along(z1=0, z2=3))
    zr2 = send(rest, along(z1=2, z2=1))
    zr4 = send(zr2, along(z1=0, z2=3))
    outer = (z == 0) | (z == TB - 1)
    slot_b = jnp.where(outer, zp4, zp2)
    slot_c = jnp.where(outer, zp5, zp3)
    y0 = send(piece, to_y)
    ya = send(zp1, to_y)
    yb = send(slot_b, to_y)
    yc = send(slot_c, to_y)
    early_pieces = [whole, y0, send(rest, to_y), zp1, send(zp1, to_x), ya, send(ya, to_x)]
    mid_pieces = [
        slot_b,
        zr4,
        zr2,
        yb,
        send(yb, to_x),
    ]
    late_pieces = [slot_c, send(slot_c, to_x), yc, send(yc, to_x)]

    quarter = width // 4
    kept, given = local_state(mine, k, v)
    from_core = send(given, to_core)
    chip = add_up(kept, from_core)
    from_y = send(chip[quarter:], to_y)
    plane = add_up(chip[:quarter], from_y)
    below = send(plane, up(1))
    two = add_up(plane, below)
    below = send(two, up(2))
    share = add_up(two, below)
    beside = send(share, to_y)
    states = [share, send(share, to_core), beside, send(beside, to_core)]
    states = [vm(s) for s in states]

    late = attend((1, 2), mine, q, states, gain)
    late_other = vm(send(late, to_core))
    early = attend((0,), mine, q, states, gain)
    early_other = vm(send(early, to_core))

    pair_rows = cols * devices // 4
    rims, taps = [], []
    for name, pieces in (("a", early_pieces), ("b", mid_pieces), ("c", late_pieces)):
        count = pair_rows if name == "a" else pair_rows // 2
        rim, w = pl.pallas_call(
            functools.partial(rim_kernel, cols, half, "abc".index(name)),
            in_specs=[SMEM] + [VMEM] * (2 + len(pieces)),
            out_specs=[VMEM] * 2,
            out_shape=[
                pltpu.VMEM((count, 4 * pixels), jnp.bfloat16),
                pltpu.VMEM((3, count, width), jnp.bfloat16),
            ],
            compiler_params=limit(16),
            name="rim",
        )(code, late, late_other, *[p if p is whole else vm(p) for p in pieces])
        rim = send(rim, up(1))
        rims += [rim, send(rim, to_core)]
        taps.append(w)
    sums = []
    for name, parts in (("a", taps[:1]), ("b", taps[1:])):
        keep, give = pl.pallas_call(
            functools.partial(own_kernel, name == "b"),
            in_specs=[SMEM] + [VMEM] * (4 + len(parts)),
            out_specs=[VMEM] * 2,
            out_shape=[pltpu.VMEM((pair_rows, 3 * pixels), jnp.float32)] * 2,
            compiler_params=limit(16),
            name="own",
        )(code, late, late_other, early, early_other, *parts)
        sums += [keep, vm(send(give, to_core))]

    result = pl.pallas_call(
        functools.partial(out_kernel, cols),
        in_specs=[SMEM] + [VMEM] * 10,
        out_specs=VMEM,
        out_shape=jax.ShapeDtypeStruct((frames, pixels, 4 * pair_rows), jnp.bfloat16),
        scratch_shapes=[pltpu.VMEM((4 * pair_rows, pixels), jnp.float32)],
        compiler_params=limit(16),
        name="out",
    )(code, *sums, *[vm(rim) for rim in rims])
    return result[None]


def solution(mesh):
    placed = (
        P(("groups", "strip"), None, None, None),
        P(("groups", "strip"), None, None, None),
        P(("groups", "strip"), None, None, None),
        P(),
        P(None, None, "strip"),
    )

    groups, devices = mesh.shape["groups"], mesh.shape["strip"]
    square = groups == 2 and devices == 4 * TB

    def per_device(queries, keys, values, norm_gain, conv_weight):
        _, frames, pixels, width = queries.shape
        cols = conv_weight.shape[2]
        fits = (
            square
            and frames == 3
            and pixels == LANES
            and width == H * DH
            and cols % 8 == 0
            and cols * devices % LANES == 0
        )
        form = tuned if fits else generic
        return form(queries, keys, values, norm_gain, conv_weight)

    return jax.shard_map(
        per_device,
        mesh=mesh,
        in_specs=placed,
        out_specs=P(("groups", "strip"), None, None, None),
        check_vma=False,
    )
```

```python
import functools

import jax
import jax.numpy as jnp
from jax import lax
from jax.experimental import pallas as pl
from jax.experimental.pallas import tpu as pltpu
from jax.sharding import PartitionSpec as P


H = 20
DH = 112
TB = 4
EPS = 1e-06
LANES = 128
ANY = pl.BlockSpec(memory_space=pl.ANY)
VMEM = pl.BlockSpec(memory_space=pltpu.VMEM)
SMEM = pl.BlockSpec(memory_space=pltpu.SMEM)


def from_behind(block, axis, distance):
    devices = range(lax.axis_size(axis))
    route = [(i - distance, i) for i in devices if i - distance in devices]
    return lax.ppermute(block, axis, route)


def generic(queries, keys, values, norm_gain, conv_weight):
    _, frames, pixels, width = queries.shape
    devices = lax.axis_size("strip")
    strips = devices // TB
    block_index = lax.axis_index("strip") // strips
    count = frames * pixels
    key_heads = jax.nn.relu(keys).reshape(count, H, DH)
    value_heads = values.reshape(count, H, DH)
    key_value = jnp.einsum(
        "nhd,nhe->hde", key_heads, value_heads, preferred_element_type=jnp.float32
    )
    key_sums = jnp.sum(key_heads, axis=0, dtype=jnp.float32)
    state_len = H * DH * DH
    raw_len = state_len + width
    row_len = (raw_len + devices - 1) // devices * devices
    row = jnp.concatenate(
        [key_value.reshape(-1), key_sums.reshape(-1), jnp.zeros((row_len - raw_len,), jnp.float32)]
    )
    later_blocks = (jnp.arange(TB) >= block_index).astype(jnp.float32)[:, None]
    share = lax.psum_scatter(later_blocks * row[None, :], "strip", scatter_dimension=1, tiled=True)
    outgoing = jnp.broadcast_to(share[:, None, :], (TB, strips, share.shape[1])).reshape(
        devices, share.shape[1]
    )
    returned = lax.all_to_all(outgoing, "strip", split_axis=0, concat_axis=1, tiled=True).reshape(
        -1
    )
    state = returned[:state_len].reshape(H, DH, DH)
    summed = returned[state_len:raw_len].reshape(H, DH)
    state_rounded = state.astype(jnp.bfloat16)
    query_heads = jax.nn.relu(queries).reshape(count, H, DH)
    numer = jnp.einsum(
        "nhd,hde->nhe", query_heads, state_rounded, preferred_element_type=jnp.float32
    )
    denom = (
        jnp.einsum(
            "nhd,hd->nh", query_heads.astype(jnp.float32), summed, precision=lax.Precision.HIGHEST
        )
        + EPS
    )
    attended = (numer / denom[..., None]).reshape(count, width)
    scale = lax.rsqrt(jnp.mean(attended * attended, axis=-1, keepdims=True) + EPS)
    normed = (attended * scale * norm_gain).astype(jnp.bfloat16).reshape(frames, pixels, width)
    rim = from_behind(normed[-2:], "strip", strips)
    extended = jnp.concatenate([rim, normed], axis=0)
    stacked = jnp.concatenate([normed, extended[1:-1], extended[:-2]], axis=-1).reshape(
        -1, 3 * width
    )
    full_taps = lax.all_gather(conv_weight, "strip", axis=2, tiled=True)
    mixed = jnp.dot(
        stacked, full_taps.reshape(3 * width, -1), preferred_element_type=jnp.float32
    ).astype(jnp.bfloat16)
    return mixed.reshape(1, frames, pixels, mixed.shape[-1])


def vm(value):
    return pltpu.with_memory_space_constraint(value, pltpu.VMEM)


def hbm(value):
    return pltpu.with_memory_space_constraint(value, pltpu.HBM)


def limit(mib):
    return pltpu.CompilerParams(vmem_limit_bytes=mib * 2**20)


def slice_kernel(step, x_ref, from_ref, to_ref, sems):
    count = to_ref.shape[0] // sems.shape[0]
    copies = []
    for i in range(sems.shape[0]):
        at = pl.ds(pl.multiple_of(x_ref[0] * step + i * count, 8), count)
        copies.append(
            pltpu.make_async_copy(
                from_ref.at[at, :], to_ref.at[pl.ds(i * count, count), :], sems.at[i]
            )
        )
    for copy in copies:
        copy.start()
    for copy in copies:
        copy.wait()


def half_of(x, whole, half):
    rows, width = whole.shape
    return pl.pallas_call(
        functools.partial(slice_kernel, rows - half),
        in_specs=[SMEM, ANY],
        out_specs=VMEM,
        out_shape=pltpu.VMEM((half, width), whole.dtype),
        scratch_shapes=[pltpu.SemaphoreType.DMA((half // 8,))],
        compiler_params=limit(4),
        name="half_of",
    )(x, hbm(whole))


def state_kernel(mine, k_ref, v_ref, *outs):
    step = pl.program_id(0)
    frames, rows, pixels = k_ref.shape
    heads = rows // DH
    fill = (lax.broadcasted_iota(jnp.int32, (LANES - DH, frames * pixels), 0) == 0).astype(
        jnp.bfloat16
    )

    for head in range(heads):
        part = pl.ds(head * DH, DH)
        k = jnp.concatenate([k_ref[f, part, :] for f in range(frames)], axis=1)
        v = jnp.concatenate([v_ref[f, part, :] for f in range(frames)], axis=1)
        k = jnp.maximum(k, jnp.zeros_like(k))
        v = jnp.concatenate([v, fill], axis=0)
        both = lax.dot_general(
            k, v, (((1,), (1,)), ((), ())), preferred_element_type=jnp.float32
        ).astype(jnp.bfloat16)
        for i, out in enumerate(outs):

            @pl.when(step % 2 == i)
            def _(out=out):
                out[part, :] = both


def local_state(mine, keys, values):
    frames, width, pixels = keys.shape
    quarter = width // 4
    spec = pl.BlockSpec((frames, quarter, pixels), lambda r, m: (0, r ^ m[0], 0))
    return pl.pallas_call(
        state_kernel,
        grid_spec=pltpu.PrefetchScalarGridSpec(
            num_scalar_prefetch=1,
            grid=(4,),
            in_specs=[spec, spec],
            out_specs=[pl.BlockSpec((quarter, LANES), lambda r, m: (r // 2, 0))] * 2,
        ),
        out_shape=[jax.ShapeDtypeStruct((2 * quarter, LANES), jnp.bfloat16)] * 2,
        name="local_state",
    )(mine, keys, values)


def add_up(*parts):
    total = parts[0].astype(jnp.float32)
    for part in parts[1:]:
        total = total + part.astype(jnp.float32)
    return total.astype(parts[0].dtype)


def attend_kernel(chosen, mine, q_ref, s0, s1, s2, s3, gain_ref, out_ref, attended):
    heads = s0.shape[0] // DH
    lanes = out_ref.shape[1]
    squares = jnp.zeros((8, lanes), jnp.float32)
    for r, state_ref in enumerate((s0, s1, s2, s3)):
        first = (r ^ mine[0]) * heads
        for i in range(heads):
            at = pl.ds(pl.multiple_of((first + i) * DH, 16), DH)
            q = jnp.concatenate([q_ref[f, at, :] for f in chosen], axis=1)
            q = jnp.maximum(q, jnp.zeros_like(q))
            s = state_ref[pl.ds(i * DH, DH), :]
            both = lax.dot_general(
                s, q, (((0,), (0,)), ((), ())), preferred_element_type=jnp.float32
            )
            a = both[:DH] * (1.0 / (both[DH : DH + 1] + EPS))
            attended[at, :] = a
            squares = squares + jnp.sum((a * a).reshape(DH // 8, 8, lanes), axis=0)
    width = attended.shape[0]
    mean = jnp.sum(squares, axis=0, keepdims=True) / width
    scale = lax.rsqrt(mean + EPS)
    for i in range(width // DH):
        at = pl.ds(i * DH, DH)
        gain = gain_ref[at, :]
        gain = jnp.concatenate([gain] * (lanes // LANES), axis=1)
        out_ref[at, :] = (attended[at, :] * scale * gain).astype(out_ref.dtype)


def attend(chosen, mine, queries, states, gain):
    _, width, pixels = queries.shape
    lanes = len(chosen) * pixels
    return pl.pallas_call(
        functools.partial(attend_kernel, chosen),
        in_specs=[SMEM] + [VMEM] * 6,
        out_specs=VMEM,
        out_shape=pltpu.VMEM((width, lanes), jnp.bfloat16),
        scratch_shapes=[pltpu.VMEM((width, lanes), jnp.float32)],
        compiler_params=limit(16),
        name="attend",
    )(mine, queries, *states, gain)


def place(x, cols, half, tap, shards, w):
    rows = 3 * cols
    lo_tap, hi_tap = tap * cols, (tap + 1) * cols

    def put(ref, slot, lo, hi, shift):
        a, b = max(lo, lo_tap), min(hi, hi_tap)
        if a < b:
            at = pl.ds(slot * cols + a - lo_tap, b - a)
            part = pl.ds(a - shift, b - a)
            w[at, :] = ref[part, :]

    for slot, shard in enumerate(shards):
        if len(shard) == 1:
            put(shard[0], slot, 0, rows, 0)

    for flag in (True, False):

        @pl.when((x == 0) == flag)
        def _(flag=flag):
            for slot, shard in enumerate(shards):
                if len(shard) == 2:
                    for ref, top in ((shard[0], flag), (shard[1], not flag)):
                        if top:
                            put(ref, slot, 0, half, 0)
                        else:
                            put(ref, slot, half, rows, rows - half)


def dot(a, b):
    return lax.dot_general(a, b, (((1,), (0,)), ((), ())), preferred_element_type=jnp.float32)


def where_of(code):
    return code // (4 * TB), code // 4 % TB, code // 2 % 2, code % 2


def blocks_of(part, z, y):
    low = z < TB // 2
    near = z ^ 1
    nearer = jnp.where(low, TB // 2, TB // 2 - 1)
    farther = jnp.where(low, TB - 1, 0)
    if part == 0:
        return [(z, y), (z, 1 - y), (near, y), (near, 1 - y), (nearer, y)]
    return [(nearer, 1 - y), (farther, y), (farther, 1 - y)]


def both_cores(own, other, at):
    return jnp.concatenate([own[:, at], other[:, at]], axis=1)


def rim_kernel(cols, half, part, code, n_own, n_other, *refs):
    pieces, (out, w) = refs[:-2], refs[-2:]
    x, _, _, _ = where_of(code[0])
    shards = []
    if part == 0:
        shards, pieces = [pieces[:1]], pieces[1:]
    shards += [pieces[i : i + 2] for i in range(0, len(pieces), 2)]
    for tap in (2, 1, 0):
        place(x, cols, half, tap, shards, w.at[tap])
    p = n_own.shape[1] // 2
    first = both_cores(n_own, n_other, pl.ds(0, p))
    last = both_cores(n_own, n_other, pl.ds(p, p))
    out[:, 2 * p :] = dot(w[2], last).astype(out.dtype)
    out[:, : 2 * p] = (dot(w[2], first) + dot(w[1], last)).astype(out.dtype)


def own_kernel(n_own, n_other, z_own, z_other, w, keep, give):
    p = n_own.shape[1] // 2
    zero = jnp.concatenate([z_own[...], z_other[...]], axis=1)
    first = both_cores(n_own, n_other, pl.ds(0, p))
    last = both_cores(n_own, n_other, pl.ds(p, p))
    totals = (
        dot(w[0], zero),
        dot(w[0], first) + dot(w[1], zero),
        dot(w[0], last) + dot(w[1], first) + dot(w[2], zero),
    )
    for f, total in enumerate(totals):
        at = pl.ds(f * p, p)
        keep[:, at], give[:, at] = total[:, :p], total[:, p:]


def out_kernel(cols, code, *refs):
    sums, rims, (out, rows) = refs[:4], refs[4:8], refs[8:]
    p = out.shape[1]
    _, z, y, core = where_of(code[0])

    def at(block, who):
        c = core if who == 0 else 1 - core
        return pl.ds(pl.multiple_of(((block[0] * 2 + block[1]) * 2 + c) * cols, 8), cols)

    for f in range(3):
        for part in range(2):
            for i, block in enumerate(blocks_of(part, z, y)):
                for who in range(2):
                    total = sums[2 * part + who][pl.ds(i * cols, cols), pl.ds(f * p, p)]
                    rows[at(block, who), :] = total
        if f < 2:
            for part in range(2):
                for i, block in enumerate(blocks_of(part, jnp.maximum(z - 1, 0), y)):
                    for who in range(2):
                        to = at(block, who)
                        rim = rims[2 * part + who][
                            pl.ds(i * cols, cols), pl.ds((2 * f + who) * p, p)
                        ]
                        rows[to, :] = rows[to, :] + rim.astype(jnp.float32)
        for j in range(rows.shape[0] // LANES):
            tile = rows[pl.ds(j * LANES, LANES), :]
            out[f, :, pl.ds(j * LANES, LANES)] = tile.T.astype(out.dtype)


def tuned(queries, keys, values, norm_gain, conv_weight):
    _, frames, pixels, width = queries.shape
    cols = conv_weight.shape[2]
    axes = ("groups", "strip")
    groups, devices = lax.axis_size("groups"), lax.axis_size("strip")
    strips = devices // TB
    x, s = lax.axis_index("groups"), lax.axis_index("strip")
    z, inside = s // strips, s % strips
    y, core = inside // 2, inside % 2

    def send(block, where):
        route = []
        for g in range(groups):
            for d in range(devices):
                to = where(g, d)
                if to is not None:
                    route.append((g * devices + d, to[0] * devices + to[1]))
        return lax.ppermute(block, axes, route)

    def to_core(g, d):
        return g, d ^ 1

    def to_y(g, d):
        return g, d ^ 2

    def to_x(g, d):
        return 1 - g, d

    def up(r):
        return lambda g, d: (g, d + r * strips) if d + r * strips < devices else None

    def along(**pairs):
        table = {int(a[1:]): b for a, b in pairs.items()}
        return lambda g, d: (
            (g, table[d // strips] * strips + d % strips) if d // strips in table else None
        )

    mine = inside.astype(jnp.int32).reshape(1)
    side = x.astype(jnp.int32).reshape(1)
    code = (x * devices // strips * 4 + z * 4 + y * 2 + core).astype(jnp.int32).reshape(1)
    k = keys[0].transpose(0, 2, 1)
    v = values[0].transpose(0, 2, 1)
    q = queries[0].transpose(0, 2, 1)
    q = vm(q)
    gain = vm(jnp.broadcast_to(norm_gain[:, None], (width, LANES)))

    rows = 3 * cols
    half = -(-rows // 16) * 8
    whole = conv_weight.transpose(0, 2, 1).reshape(rows, width)
    piece = half_of(side, whole, half)
    rest = half_of(1 - side, whole, half)
    zp1 = send(piece, along(z0=1, z1=0, z2=3, z3=2))
    zp2 = send(piece, along(z1=2, z2=1))
    zp3 = send(zp1, along(z1=2, z2=1))
    zp4 = send(zp2, along(z1=0, z2=3))
    zp5 = send(zp3, along(z1=0, z2=3))
    zr2 = send(rest, along(z1=2, z2=1))
    zr4 = send(zr2, along(z1=0, z2=3))
    outer = (z == 0) | (z == TB - 1)
    slot_b = jnp.where(outer, zp4, zp2)
    rest_b = jnp.where(outer, zr4, zr2)
    slot_c = jnp.where(outer, zp5, zp3)
    y0 = send(piece, to_y)
    ya = send(zp1, to_y)
    yb = send(slot_b, to_y)
    yc = send(slot_c, to_y)
    early_pieces = [
        whole, y0, send(y0, to_x), zp1, send(zp1, to_x), ya, send(ya, to_x), slot_b, rest_b
    ]
    late_pieces = [yb, send(rest_b, to_y), slot_c, send(slot_c, to_x), yc, send(yc, to_x)]

    quarter = width // 4
    kept, given = local_state(mine, k, v)
    from_core = send(given, to_core)
    chip = add_up(kept, from_core)
    from_y = send(chip[quarter:], to_y)
    plane = add_up(chip[:quarter], from_y)
    below = send(plane, up(1))
    two = add_up(plane, below)
    below = send(two, up(2))
    share = add_up(two, below)
    beside = send(share, to_y)
    states = [share, send(share, to_core), beside, send(beside, to_core)]
    states = [vm(s) for s in states]

    late = attend((1, 2), mine, q, states, gain)
    late_other = vm(send(late, to_core))
    early = attend((0,), mine, q, states, gain)
    early_other = vm(send(early, to_core))

    sums, rims = [], []
    for name, pieces in (("a", early_pieces), ("b", late_pieces)):
        count = cols * len(blocks_of("ab".index(name), z, y))
        rim, w = pl.pallas_call(
            functools.partial(rim_kernel, cols, half, "ab".index(name)),
            in_specs=[SMEM] + [VMEM] * (2 + len(pieces)),
            out_specs=[VMEM] * 2,
            out_shape=[
                pltpu.VMEM((count, 4 * pixels), jnp.bfloat16),
                pltpu.VMEM((3, count, width), jnp.bfloat16),
            ],
            compiler_params=limit(16),
            name="rim",
        )(code, late, late_other, *[p if p is whole else vm(p) for p in pieces])
        rim = send(rim, up(1))
        rims += [rim, send(rim, to_core)]
        keep, give = pl.pallas_call(
            own_kernel,
            in_specs=[VMEM] * 5,
            out_specs=[VMEM] * 2,
            out_shape=[pltpu.VMEM((count, 3 * pixels), jnp.float32)] * 2,
            compiler_params=limit(16),
            name="own",
        )(late, late_other, early, early_other, w)
        sums += [keep, vm(send(give, to_core))]

    result = pl.pallas_call(
        functools.partial(out_kernel, cols),
        in_specs=[SMEM] + [VMEM] * 8,
        out_specs=VMEM,
        out_shape=jax.ShapeDtypeStruct((frames, pixels, cols * devices), jnp.bfloat16),
        scratch_shapes=[pltpu.VMEM((cols * devices, pixels), jnp.float32)],
        compiler_params=limit(16),
        name="out",
    )(code, *sums, *[vm(rim) for rim in rims])
    return result[None]


def solution(mesh):
    placed = (
        P(("groups", "strip"), None, None, None),
        P(("groups", "strip"), None, None, None),
        P(("groups", "strip"), None, None, None),
        P(),
        P(None, None, "strip"),
    )

    groups, devices = mesh.shape["groups"], mesh.shape["strip"]
    square = groups == 2 and devices == 4 * TB

    def per_device(queries, keys, values, norm_gain, conv_weight):
        _, frames, pixels, width = queries.shape
        cols = conv_weight.shape[2]
        fits = (
            square
            and frames == 3
            and pixels == LANES
            and width == H * DH
            and cols % 8 == 0
            and cols * devices % LANES == 0
        )
        form = tuned if fits else generic
        return form(queries, keys, values, norm_gain, conv_weight)

    return jax.shard_map(
        per_device,
        mesh=mesh,
        in_specs=placed,
        out_specs=P(("groups", "strip"), None, None, None),
        check_vma=False,
    )
```

```python
import functools

import jax
import jax.numpy as jnp
from jax import lax
from jax.experimental import pallas as pl
from jax.experimental.pallas import tpu as pltpu
from jax.sharding import PartitionSpec as P


H = 20
DH = 112
TB = 4
EPS = 1e-06
LANES = 128
ANY = pl.BlockSpec(memory_space=pl.ANY)
VMEM = pl.BlockSpec(memory_space=pltpu.VMEM)
SMEM = pl.BlockSpec(memory_space=pltpu.SMEM)


def from_behind(block, axis, distance):
    devices = range(lax.axis_size(axis))
    route = [(i - distance, i) for i in devices if i - distance in devices]
    return lax.ppermute(block, axis, route)


def generic(queries, keys, values, norm_gain, conv_weight):
    _, frames, pixels, width = queries.shape
    devices = lax.axis_size("strip")
    strips = devices // TB
    block_index = lax.axis_index("strip") // strips
    count = frames * pixels
    key_heads = jax.nn.relu(keys).reshape(count, H, DH)
    value_heads = values.reshape(count, H, DH)
    key_value = jnp.einsum(
        "nhd,nhe->hde", key_heads, value_heads, preferred_element_type=jnp.float32
    )
    key_sums = jnp.sum(key_heads, axis=0, dtype=jnp.float32)
    state_len = H * DH * DH
    raw_len = state_len + width
    row_len = (raw_len + devices - 1) // devices * devices
    row = jnp.concatenate(
        [key_value.reshape(-1), key_sums.reshape(-1), jnp.zeros((row_len - raw_len,), jnp.float32)]
    )
    later_blocks = (jnp.arange(TB) >= block_index).astype(jnp.float32)[:, None]
    share = lax.psum_scatter(later_blocks * row[None, :], "strip", scatter_dimension=1, tiled=True)
    outgoing = jnp.broadcast_to(share[:, None, :], (TB, strips, share.shape[1])).reshape(
        devices, share.shape[1]
    )
    returned = lax.all_to_all(outgoing, "strip", split_axis=0, concat_axis=1, tiled=True).reshape(
        -1
    )
    state = returned[:state_len].reshape(H, DH, DH)
    summed = returned[state_len:raw_len].reshape(H, DH)
    state_rounded = state.astype(jnp.bfloat16)
    query_heads = jax.nn.relu(queries).reshape(count, H, DH)
    numer = jnp.einsum(
        "nhd,hde->nhe", query_heads, state_rounded, preferred_element_type=jnp.float32
    )
    denom = (
        jnp.einsum(
            "nhd,hd->nh", query_heads.astype(jnp.float32), summed, precision=lax.Precision.HIGHEST
        )
        + EPS
    )
    attended = (numer / denom[..., None]).reshape(count, width)
    scale = lax.rsqrt(jnp.mean(attended * attended, axis=-1, keepdims=True) + EPS)
    normed = (attended * scale * norm_gain).astype(jnp.bfloat16).reshape(frames, pixels, width)
    rim = from_behind(normed[-2:], "strip", strips)
    extended = jnp.concatenate([rim, normed], axis=0)
    stacked = jnp.concatenate([normed, extended[1:-1], extended[:-2]], axis=-1).reshape(
        -1, 3 * width
    )
    full_taps = lax.all_gather(conv_weight, "strip", axis=2, tiled=True)
    mixed = jnp.dot(
        stacked, full_taps.reshape(3 * width, -1), preferred_element_type=jnp.float32
    ).astype(jnp.bfloat16)
    return mixed.reshape(1, frames, pixels, mixed.shape[-1])


def vm(value):
    return pltpu.with_memory_space_constraint(value, pltpu.VMEM)


def hbm(value):
    return pltpu.with_memory_space_constraint(value, pltpu.HBM)


def limit(mib):
    return pltpu.CompilerParams(vmem_limit_bytes=mib * 2**20)


def slice_kernel(step, x_ref, from_ref, to_ref, sems):
    count = to_ref.shape[0] // sems.shape[0]
    copies = []
    for i in range(sems.shape[0]):
        at = pl.ds(pl.multiple_of(x_ref[0] * step + i * count, 8), count)
        copies.append(
            pltpu.make_async_copy(
                from_ref.at[at, :], to_ref.at[pl.ds(i * count, count), :], sems.at[i]
            )
        )
    for copy in copies:
        copy.start()
    for copy in copies:
        copy.wait()


def half_of(x, whole, half):
    rows, width = whole.shape
    return pl.pallas_call(
        functools.partial(slice_kernel, rows - half),
        in_specs=[SMEM, ANY],
        out_specs=VMEM,
        out_shape=pltpu.VMEM((half, width), whole.dtype),
        scratch_shapes=[pltpu.SemaphoreType.DMA((half // 8,))],
        compiler_params=limit(4),
        name="half_of",
    )(x, hbm(whole))


def pick_kernel(flag, a, b, out):
    @pl.when(flag[0] == 1)
    def _():
        out[...] = a[...]

    @pl.when(flag[0] == 0)
    def _():
        out[...] = b[...]


def pick(flag, a, b):
    return pl.pallas_call(
        pick_kernel,
        in_specs=[SMEM, VMEM, VMEM],
        out_specs=VMEM,
        out_shape=pltpu.VMEM(a.shape, a.dtype),
        compiler_params=limit(4),
        name="pick",
    )(flag, a, b)


def state_kernel(mine, k_ref, v_ref, *outs):
    step = pl.program_id(0)
    frames, rows, pixels = k_ref.shape
    heads = rows // DH
    fill = (lax.broadcasted_iota(jnp.int32, (LANES - DH, frames * pixels), 0) == 0).astype(
        jnp.bfloat16
    )

    for head in range(heads):
        part = pl.ds(head * DH, DH)
        k = jnp.concatenate([k_ref[f, part, :] for f in range(frames)], axis=1)
        v = jnp.concatenate([v_ref[f, part, :] for f in range(frames)], axis=1)
        k = jnp.maximum(k, jnp.zeros_like(k))
        v = jnp.concatenate([v, fill], axis=0)
        both = lax.dot_general(
            k, v, (((1,), (1,)), ((), ())), preferred_element_type=jnp.float32
        ).astype(jnp.bfloat16)
        for i, out in enumerate(outs):

            @pl.when(step % 2 == i)
            def _(out=out):
                out[part, :] = both


def local_state(mine, keys, values):
    frames, width, pixels = keys.shape
    quarter = width // 4
    spec = pl.BlockSpec((frames, quarter, pixels), lambda r, m: (0, r ^ m[0], 0))
    return pl.pallas_call(
        state_kernel,
        grid_spec=pltpu.PrefetchScalarGridSpec(
            num_scalar_prefetch=1,
            grid=(4,),
            in_specs=[spec, spec],
            out_specs=[pl.BlockSpec((quarter, LANES), lambda r, m: (r // 2, 0))] * 2,
        ),
        out_shape=[jax.ShapeDtypeStruct((2 * quarter, LANES), jnp.bfloat16)] * 2,
        name="local_state",
    )(mine, keys, values)


def add_up(*parts):
    total = parts[0].astype(jnp.float32)
    for part in parts[1:]:
        total = total + part.astype(jnp.float32)
    return total.astype(parts[0].dtype)


def attend_kernel(chosen, mine, q_ref, s0, s1, s2, s3, gain_ref, out_ref, attended):
    heads = s0.shape[0] // DH
    lanes = out_ref.shape[1]
    squares = jnp.zeros((8, lanes), jnp.float32)
    for r, state_ref in enumerate((s0, s1, s2, s3)):
        first = (r ^ mine[0]) * heads
        for i in range(heads):
            at = pl.ds(pl.multiple_of((first + i) * DH, 16), DH)
            q = jnp.concatenate([q_ref[f, at, :] for f in chosen], axis=1)
            q = jnp.maximum(q, jnp.zeros_like(q))
            s = state_ref[pl.ds(i * DH, DH), :]
            both = lax.dot_general(
                s, q, (((0,), (0,)), ((), ())), preferred_element_type=jnp.float32
            )
            a = both[:DH] * (1.0 / (both[DH : DH + 1] + EPS))
            attended[at, :] = a
            squares = squares + jnp.sum((a * a).reshape(DH // 8, 8, lanes), axis=0)
    width = attended.shape[0]
    mean = jnp.sum(squares, axis=0, keepdims=True) / width
    scale = lax.rsqrt(mean + EPS)
    for i in range(width // DH):
        at = pl.ds(i * DH, DH)
        gain = gain_ref[at, :]
        gain = jnp.concatenate([gain] * (lanes // LANES), axis=1)
        out_ref[at, :] = (attended[at, :] * scale * gain).astype(out_ref.dtype)


def attend(chosen, mine, queries, states, gain):
    _, width, pixels = queries.shape
    lanes = len(chosen) * pixels
    return pl.pallas_call(
        functools.partial(attend_kernel, chosen),
        in_specs=[SMEM] + [VMEM] * 6,
        out_specs=VMEM,
        out_shape=pltpu.VMEM((width, lanes), jnp.bfloat16),
        scratch_shapes=[pltpu.VMEM((width, lanes), jnp.float32)],
        compiler_params=limit(16),
        name="attend",
    )(mine, queries, *states, gain)


def place(x, cols, half, tap, shards, w):
    rows = 3 * cols
    lo_tap, hi_tap = tap * cols, (tap + 1) * cols

    def put(ref, slot, lo, hi, shift):
        a, b = max(lo, lo_tap), min(hi, hi_tap)
        if a < b:
            at = pl.ds(slot * cols + a - lo_tap, b - a)
            part = pl.ds(a - shift, b - a)
            w[at, :] = ref[part, :]

    for slot, shard in enumerate(shards):
        if len(shard) == 1:
            put(shard[0], slot, 0, rows, 0)

    for flag in (True, False):

        @pl.when((x == 0) == flag)
        def _(flag=flag):
            for slot, shard in enumerate(shards):
                if len(shard) == 2:
                    for ref, top in ((shard[0], flag), (shard[1], not flag)):
                        if top:
                            put(ref, slot, 0, half, 0)
                        else:
                            put(ref, slot, half, rows, rows - half)


def dot(a, b):
    return lax.dot_general(a, b, (((1,), (0,)), ((), ())), preferred_element_type=jnp.float32)


def where_of(code):
    return code // (4 * TB), code // 4 % TB, code // 2 % 2, code % 2


def blocks_of(part, z, y):
    low = z < TB // 2
    near = z ^ 1
    nearer = jnp.where(low, TB // 2, TB // 2 - 1)
    farther = jnp.where(low, TB - 1, 0)
    if part == 0:
        return [(z, y), (z, 1 - y), (near, y), (near, 1 - y), (nearer, y), (farther, y)]
    return [(nearer, 1 - y), (farther, 1 - y)]


def both_cores(own, other, at):
    return jnp.concatenate([own[:, at], other[:, at]], axis=1)


def rim_kernel(cols, half, part, code, n_own, n_other, *refs):
    pieces, (out, w) = refs[:-2], refs[-2:]
    x, _, _, _ = where_of(code[0])
    shards = []
    if part == 0:
        shards, pieces = [pieces[:1]], pieces[1:]
    shards += [pieces[i : i + 2] for i in range(0, len(pieces), 2)]
    for tap in (2, 1, 0):
        place(x, cols, half, tap, shards, w.at[tap])
    p = n_own.shape[1] // 2
    first = both_cores(n_own, n_other, pl.ds(0, p))
    last = both_cores(n_own, n_other, pl.ds(p, p))
    out[:, 2 * p :] = dot(w[2], last).astype(out.dtype)
    out[:, : 2 * p] = (dot(w[2], first) + dot(w[1], last)).astype(out.dtype)


def own_kernel(n_own, n_other, z_own, z_other, w, keep, give):
    p = n_own.shape[1] // 2
    zero = jnp.concatenate([z_own[...], z_other[...]], axis=1)
    first = both_cores(n_own, n_other, pl.ds(0, p))
    last = both_cores(n_own, n_other, pl.ds(p, p))
    totals = (
        dot(w[0], zero),
        dot(w[0], first) + dot(w[1], zero),
        dot(w[0], last) + dot(w[1], first) + dot(w[2], zero),
    )
    for f, total in enumerate(totals):
        at = pl.ds(f * p, p)
        keep[:, at], give[:, at] = total[:, :p], total[:, p:]


def out_kernel(cols, code, *refs):
    sums, rims, (out, rows) = refs[:4], refs[4:8], refs[8:]
    p = out.shape[1]
    _, z, y, core = where_of(code[0])

    def at(block, who):
        c = core if who == 0 else 1 - core
        return pl.ds(pl.multiple_of(((block[0] * 2 + block[1]) * 2 + c) * cols, 8), cols)

    for f in range(3):
        for part in range(2):
            for i, block in enumerate(blocks_of(part, z, y)):
                for who in range(2):
                    total = sums[2 * part + who][pl.ds(i * cols, cols), pl.ds(f * p, p)]
                    rows[at(block, who), :] = total
        if f < 2:
            for part in range(2):
                for i, block in enumerate(blocks_of(part, jnp.maximum(z - 1, 0), y)):
                    for who in range(2):
                        to = at(block, who)
                        rim = rims[2 * part + who][
                            pl.ds(i * cols, cols), pl.ds((2 * f + who) * p, p)
                        ]
                        rows[to, :] = rows[to, :] + rim.astype(jnp.float32)
        for j in range(rows.shape[0] // LANES):
            tile = rows[pl.ds(j * LANES, LANES), :]
            out[f, :, pl.ds(j * LANES, LANES)] = tile.T.astype(out.dtype)


def tuned(queries, keys, values, norm_gain, conv_weight):
    _, frames, pixels, width = queries.shape
    cols = conv_weight.shape[2]
    axes = ("groups", "strip")
    groups, devices = lax.axis_size("groups"), lax.axis_size("strip")
    strips = devices // TB
    x, s = lax.axis_index("groups"), lax.axis_index("strip")
    z, inside = s // strips, s % strips
    y, core = inside // 2, inside % 2

    def send(block, where):
        route = []
        for g in range(groups):
            for d in range(devices):
                to = where(g, d)
                if to is not None:
                    route.append((g * devices + d, to[0] * devices + to[1]))
        moved = lax.ppermute(block, axes, route)
        return vm(moved) if block.shape[1] == width else moved

    def to_core(g, d):
        return g, d ^ 1

    def to_y(g, d):
        return g, d ^ 2

    def to_x(g, d):
        return 1 - g, d

    def up(r):
        return lambda g, d: (g, d + r * strips) if d + r * strips < devices else None

    def along(**pairs):
        table = {int(a[1:]): b for a, b in pairs.items()}
        return lambda g, d: (
            (g, table[d // strips] * strips + d % strips) if d // strips in table else None
        )

    mine = inside.astype(jnp.int32).reshape(1)
    side = x.astype(jnp.int32).reshape(1)
    code = (x * devices // strips * 4 + z * 4 + y * 2 + core).astype(jnp.int32).reshape(1)
    k = keys[0].transpose(0, 2, 1)
    v = values[0].transpose(0, 2, 1)
    q = queries[0].transpose(0, 2, 1)
    q = vm(q)
    gain = vm(jnp.broadcast_to(norm_gain[:, None], (width, LANES)))

    rows = 3 * cols
    half = -(-rows // 16) * 8
    whole = conv_weight.transpose(0, 2, 1).reshape(rows, width)
    piece = half_of(side, whole, half)
    rest = half_of(1 - side, whole, half)
    zp1 = send(piece, along(z0=1, z1=0, z2=3, z3=2))
    zp2 = send(piece, along(z1=2, z2=1))
    zp3 = send(zp1, along(z1=2, z2=1))
    zp4 = send(zp2, along(z1=0, z2=3))
    zp5 = send(zp3, along(z1=0, z2=3))
    zr2 = send(rest, along(z1=2, z2=1))
    zr4 = send(zr2, along(z1=0, z2=3))
    outer = ((z == 0) | (z == TB - 1)).astype(jnp.int32).reshape(1)
    slot_b = pick(outer, zp4, zp2)
    rest_b = pick(outer, zr4, zr2)
    slot_c = pick(outer, zp5, zp3)
    y0 = send(piece, to_y)
    ya = send(zp1, to_y)
    yb = send(slot_b, to_y)
    yc = send(slot_c, to_y)
    early_pieces = [
        whole,
        y0,
        send(y0, to_x),
        zp1,
        send(zp1, to_x),
        ya,
        send(ya, to_x),
        slot_b,
        rest_b,
        slot_c,
        send(slot_c, to_x),
    ]
    late_pieces = [yb, send(rest_b, to_y), yc, send(yc, to_x)]

    quarter = width // 4
    kept, given = local_state(mine, k, v)
    from_core = send(given, to_core)
    chip = add_up(kept, from_core)
    from_y = send(chip[quarter:], to_y)
    plane = add_up(chip[:quarter], from_y)
    below = send(plane, up(1))
    two = add_up(plane, below)
    below = send(two, up(2))
    share = add_up(two, below)
    beside = send(share, to_y)
    states = [share, send(share, to_core), beside, send(beside, to_core)]
    states = [vm(s) for s in states]

    late = attend((1, 2), mine, q, states, gain)
    late_other = vm(send(late, to_core))
    early = attend((0,), mine, q, states, gain)
    early_other = vm(send(early, to_core))

    sums, rims = [], []
    for name, pieces in (("a", early_pieces), ("b", late_pieces)):
        count = cols * len(blocks_of("ab".index(name), z, y))
        rim, w = pl.pallas_call(
            functools.partial(rim_kernel, cols, half, "ab".index(name)),
            in_specs=[SMEM] + [VMEM] * (2 + len(pieces)),
            out_specs=[VMEM] * 2,
            out_shape=[
                pltpu.VMEM((count, 4 * pixels), jnp.bfloat16),
                pltpu.VMEM((3, count, width), jnp.bfloat16),
            ],
            compiler_params=limit(16),
            name="rim",
        )(code, late, late_other, *pieces)
        rim = send(rim, up(1))
        rims += [rim, send(rim, to_core)]
        keep, give = pl.pallas_call(
            own_kernel,
            in_specs=[VMEM] * 5,
            out_specs=[VMEM] * 2,
            out_shape=[pltpu.VMEM((count, 3 * pixels), jnp.float32)] * 2,
            compiler_params=limit(16),
            name="own",
        )(late, late_other, early, early_other, w)
        sums += [keep, vm(send(give, to_core))]

    result = pl.pallas_call(
        functools.partial(out_kernel, cols),
        in_specs=[SMEM] + [VMEM] * 8,
        out_specs=VMEM,
        out_shape=jax.ShapeDtypeStruct((frames, pixels, cols * devices), jnp.bfloat16),
        scratch_shapes=[pltpu.VMEM((cols * devices, pixels), jnp.float32)],
        compiler_params=limit(16),
        name="out",
    )(code, *sums, *[vm(rim) for rim in rims])
    return result[None]


def solution(mesh):
    placed = (
        P(("groups", "strip"), None, None, None),
        P(("groups", "strip"), None, None, None),
        P(("groups", "strip"), None, None, None),
        P(),
        P(None, None, "strip"),
    )

    groups, devices = mesh.shape["groups"], mesh.shape["strip"]
    square = groups == 2 and devices == 4 * TB

    def per_device(queries, keys, values, norm_gain, conv_weight):
        _, frames, pixels, width = queries.shape
        cols = conv_weight.shape[2]
        fits = (
            square
            and frames == 3
            and pixels == LANES
            and width == H * DH
            and cols % 8 == 0
            and cols * devices % LANES == 0
        )
        form = tuned if fits else generic
        return form(queries, keys, values, norm_gain, conv_weight)

    return jax.shard_map(
        per_device,
        mesh=mesh,
        in_specs=placed,
        out_specs=P(("groups", "strip"), None, None, None),
        check_vma=False,
    )
```

```python
import functools

import jax
import jax.numpy as jnp
from jax import lax
from jax.experimental import pallas as pl
from jax.experimental.pallas import tpu as pltpu
from jax.sharding import PartitionSpec as P


H = 20
DH = 112
TB = 4
EPS = 1e-06
LANES = 128
ANY = pl.BlockSpec(memory_space=pl.ANY)
VMEM = pl.BlockSpec(memory_space=pltpu.VMEM)
SMEM = pl.BlockSpec(memory_space=pltpu.SMEM)


def from_behind(block, axis, distance):
    devices = range(lax.axis_size(axis))
    route = [(i - distance, i) for i in devices if i - distance in devices]
    return lax.ppermute(block, axis, route)


def generic(queries, keys, values, norm_gain, conv_weight):
    _, frames, pixels, width = queries.shape
    devices = lax.axis_size("strip")
    strips = devices // TB
    block_index = lax.axis_index("strip") // strips
    count = frames * pixels
    key_heads = jax.nn.relu(keys).reshape(count, H, DH)
    value_heads = values.reshape(count, H, DH)
    key_value = jnp.einsum(
        "nhd,nhe->hde", key_heads, value_heads, preferred_element_type=jnp.float32
    )
    key_sums = jnp.sum(key_heads, axis=0, dtype=jnp.float32)
    state_len = H * DH * DH
    raw_len = state_len + width
    row_len = (raw_len + devices - 1) // devices * devices
    row = jnp.concatenate(
        [key_value.reshape(-1), key_sums.reshape(-1), jnp.zeros((row_len - raw_len,), jnp.float32)]
    )
    later_blocks = (jnp.arange(TB) >= block_index).astype(jnp.float32)[:, None]
    share = lax.psum_scatter(later_blocks * row[None, :], "strip", scatter_dimension=1, tiled=True)
    outgoing = jnp.broadcast_to(share[:, None, :], (TB, strips, share.shape[1])).reshape(
        devices, share.shape[1]
    )
    returned = lax.all_to_all(outgoing, "strip", split_axis=0, concat_axis=1, tiled=True).reshape(
        -1
    )
    state = returned[:state_len].reshape(H, DH, DH)
    summed = returned[state_len:raw_len].reshape(H, DH)
    state_rounded = state.astype(jnp.bfloat16)
    query_heads = jax.nn.relu(queries).reshape(count, H, DH)
    numer = jnp.einsum(
        "nhd,hde->nhe", query_heads, state_rounded, preferred_element_type=jnp.float32
    )
    denom = (
        jnp.einsum(
            "nhd,hd->nh", query_heads.astype(jnp.float32), summed, precision=lax.Precision.HIGHEST
        )
        + EPS
    )
    attended = (numer / denom[..., None]).reshape(count, width)
    scale = lax.rsqrt(jnp.mean(attended * attended, axis=-1, keepdims=True) + EPS)
    normed = (attended * scale * norm_gain).astype(jnp.bfloat16).reshape(frames, pixels, width)
    rim = from_behind(normed[-2:], "strip", strips)
    extended = jnp.concatenate([rim, normed], axis=0)
    stacked = jnp.concatenate([normed, extended[1:-1], extended[:-2]], axis=-1).reshape(
        -1, 3 * width
    )
    full_taps = lax.all_gather(conv_weight, "strip", axis=2, tiled=True)
    mixed = jnp.dot(
        stacked, full_taps.reshape(3 * width, -1), preferred_element_type=jnp.float32
    ).astype(jnp.bfloat16)
    return mixed.reshape(1, frames, pixels, mixed.shape[-1])


def vm(value):
    return pltpu.with_memory_space_constraint(value, pltpu.VMEM)


def hbm(value):
    return pltpu.with_memory_space_constraint(value, pltpu.HBM)


def limit(mib):
    return pltpu.CompilerParams(vmem_limit_bytes=mib * 2**20)


def slice_kernel(step, x_ref, from_ref, to_ref, sems):
    count = to_ref.shape[0] // sems.shape[0]
    copies = []
    for i in range(sems.shape[0]):
        at = pl.ds(pl.multiple_of(x_ref[0] * step + i * count, 8), count)
        copies.append(
            pltpu.make_async_copy(
                from_ref.at[at, :], to_ref.at[pl.ds(i * count, count), :], sems.at[i]
            )
        )
    for copy in copies:
        copy.start()
    for copy in copies:
        copy.wait()


def half_of(x, whole, half, step):
    width = whole.shape[1]
    return pl.pallas_call(
        functools.partial(slice_kernel, step),
        in_specs=[SMEM, ANY],
        out_specs=VMEM,
        out_shape=pltpu.VMEM((half, width), whole.dtype),
        scratch_shapes=[pltpu.SemaphoreType.DMA((half // 8,))],
        compiler_params=limit(4),
        name="half_of",
    )(x, hbm(whole))


def pick_kernel(flag, a, b, out):
    @pl.when(flag[0] == 1)
    def _():
        out[...] = a[...]

    @pl.when(flag[0] == 0)
    def _():
        out[...] = b[...]


def pick(flag, a, b):
    return pl.pallas_call(
        pick_kernel,
        in_specs=[SMEM, VMEM, VMEM],
        out_specs=VMEM,
        out_shape=pltpu.VMEM(a.shape, a.dtype),
        compiler_params=limit(4),
        name="pick",
    )(flag, a, b)


def state_kernel(mine, k_ref, v_ref, *outs):
    step = pl.program_id(0)
    frames, rows, pixels = k_ref.shape
    heads = rows // DH
    fill = (lax.broadcasted_iota(jnp.int32, (LANES - DH, frames * pixels), 0) == 0).astype(
        jnp.bfloat16
    )

    for head in range(heads):
        part = pl.ds(head * DH, DH)
        k = jnp.concatenate([k_ref[f, part, :] for f in range(frames)], axis=1)
        v = jnp.concatenate([v_ref[f, part, :] for f in range(frames)], axis=1)
        k = jnp.maximum(k, jnp.zeros_like(k))
        v = jnp.concatenate([v, fill], axis=0)
        both = lax.dot_general(
            k, v, (((1,), (1,)), ((), ())), preferred_element_type=jnp.float32
        ).astype(jnp.bfloat16)
        for i, out in enumerate(outs):

            @pl.when(step % 2 == i)
            def _(out=out):
                out[part, :] = both


def local_state(mine, keys, values):
    frames, width, pixels = keys.shape
    quarter = width // 4
    spec = pl.BlockSpec((frames, quarter, pixels), lambda r, m: (0, r ^ m[0], 0))
    return pl.pallas_call(
        state_kernel,
        grid_spec=pltpu.PrefetchScalarGridSpec(
            num_scalar_prefetch=1,
            grid=(4,),
            in_specs=[spec, spec],
            out_specs=[pl.BlockSpec((quarter, LANES), lambda r, m: (r // 2, 0))] * 2,
        ),
        out_shape=[jax.ShapeDtypeStruct((2 * quarter, LANES), jnp.bfloat16)] * 2,
        name="local_state",
    )(mine, keys, values)


def add_up(*parts):
    total = parts[0].astype(jnp.float32)
    for part in parts[1:]:
        total = total + part.astype(jnp.float32)
    return total.astype(parts[0].dtype)


def attend_kernel(chosen, mine, q_ref, s0, s1, s2, s3, gain_ref, out_ref, attended):
    heads = s0.shape[0] // DH
    lanes = out_ref.shape[1]
    squares = jnp.zeros((8, lanes), jnp.float32)
    for r, state_ref in enumerate((s0, s1, s2, s3)):
        first = (r ^ mine[0]) * heads
        for i in range(heads):
            at = pl.ds(pl.multiple_of((first + i) * DH, 16), DH)
            q = jnp.concatenate([q_ref[f, at, :] for f in chosen], axis=1)
            q = jnp.maximum(q, jnp.zeros_like(q))
            s = state_ref[pl.ds(i * DH, DH), :]
            both = lax.dot_general(
                s, q, (((0,), (0,)), ((), ())), preferred_element_type=jnp.float32
            )
            a = both[:DH] * (1.0 / (both[DH : DH + 1] + EPS))
            attended[at, :] = a
            squares = squares + jnp.sum((a * a).reshape(DH // 8, 8, lanes), axis=0)
    width = attended.shape[0]
    mean = jnp.sum(squares, axis=0, keepdims=True) / width
    scale = lax.rsqrt(mean + EPS)
    for i in range(width // DH):
        at = pl.ds(i * DH, DH)
        gain = gain_ref[at, :]
        gain = jnp.concatenate([gain] * (lanes // LANES), axis=1)
        out_ref[at, :] = (attended[at, :] * scale * gain).astype(out_ref.dtype)


def attend(chosen, mine, queries, states, gain):
    _, width, pixels = queries.shape
    lanes = len(chosen) * pixels
    return pl.pallas_call(
        functools.partial(attend_kernel, chosen),
        in_specs=[SMEM] + [VMEM] * 6,
        out_specs=VMEM,
        out_shape=pltpu.VMEM((width, lanes), jnp.bfloat16),
        scratch_shapes=[pltpu.VMEM((width, lanes), jnp.float32)],
        compiler_params=limit(16),
        name="attend",
    )(mine, queries, *states, gain)


def place(x, cols, tap, shards, w):
    rows = 3 * cols
    lo_tap, hi_tap = tap * cols, (tap + 1) * cols

    def put(ref, slot, lo, hi, shift):
        a, b = max(lo, lo_tap), min(hi, hi_tap)
        if a < b:
            at = pl.ds(slot * cols + a - lo_tap, b - a)
            part = pl.ds(a - shift, b - a)
            w[at, :] = ref[part, :]

    for slot, shard in enumerate(shards):
        if len(shard) == 1:
            put(shard[0], slot, 0, rows, 0)

    for flag in (True, False):

        @pl.when((x == 0) == flag)
        def _(flag=flag):
            for slot, shard in enumerate(shards):
                if len(shard) == 2:
                    top, bottom = shard if flag else shard[::-1]
                    count = bottom.shape[0]
                    put(top, slot, 0, top.shape[0], 0)
                    put(bottom, slot, rows - count, rows, rows - count)


def dot(a, b):
    return lax.dot_general(a, b, (((1,), (0,)), ((), ())), preferred_element_type=jnp.float32)


def where_of(code):
    return code // (4 * TB), code // 4 % TB, code // 2 % 2, code % 2


def blocks_of(part, z, y):
    low = z < TB // 2
    near = z ^ 1
    nearer = jnp.where(low, TB // 2, TB // 2 - 1)
    farther = jnp.where(low, TB - 1, 0)
    if part == 0:
        return [(z, y), (z, 1 - y), (near, y), (near, 1 - y), (nearer, y), (farther, y)]
    return [(nearer, 1 - y), (farther, 1 - y)]


def both_cores(own, other, at):
    return jnp.concatenate([own[:, at], other[:, at]], axis=1)


def rim_kernel(cols, part, code, n_own, n_other, *refs):
    pieces, (out, w) = refs[:-2], refs[-2:]
    x, _, _, _ = where_of(code[0])
    shards = []
    if part == 0:
        shards, pieces = [pieces[:1]], pieces[1:]
    shards += [pieces[i : i + 2] for i in range(0, len(pieces), 2)]
    for tap in (2, 1, 0):
        place(x, cols, tap, shards, w.at[tap])
    p = n_own.shape[1] // 2
    first = both_cores(n_own, n_other, pl.ds(0, p))
    last = both_cores(n_own, n_other, pl.ds(p, p))
    out[:, 2 * p :] = dot(w[2], last).astype(out.dtype)
    out[:, : 2 * p] = (dot(w[2], first) + dot(w[1], last)).astype(out.dtype)


def own_kernel(n_own, n_other, z_own, z_other, w, keep, give):
    p = n_own.shape[1] // 2
    zero = jnp.concatenate([z_own[...], z_other[...]], axis=1)
    first = both_cores(n_own, n_other, pl.ds(0, p))
    last = both_cores(n_own, n_other, pl.ds(p, p))
    totals = (
        dot(w[0], zero),
        dot(w[0], first) + dot(w[1], zero),
        dot(w[0], last) + dot(w[1], first) + dot(w[2], zero),
    )
    for f, total in enumerate(totals):
        at = pl.ds(f * p, p)
        keep[:, at], give[:, at] = total[:, :p], total[:, p:]


def out_kernel(cols, code, *refs):
    sums, rims, (out, rows) = refs[:4], refs[4:8], refs[8:]
    p = out.shape[1]
    _, z, y, core = where_of(code[0])

    def at(block, who):
        c = core if who == 0 else 1 - core
        return pl.ds(pl.multiple_of(((block[0] * 2 + block[1]) * 2 + c) * cols, 8), cols)

    for f in range(3):
        for part in range(2):
            for i, block in enumerate(blocks_of(part, z, y)):
                for who in range(2):
                    total = sums[2 * part + who][pl.ds(i * cols, cols), pl.ds(f * p, p)]
                    rows[at(block, who), :] = total
        if f < 2:
            for part in range(2):
                for i, block in enumerate(blocks_of(part, jnp.maximum(z - 1, 0), y)):
                    for who in range(2):
                        to = at(block, who)
                        rim = rims[2 * part + who][
                            pl.ds(i * cols, cols), pl.ds((2 * f + who) * p, p)
                        ]
                        rows[to, :] = rows[to, :] + rim.astype(jnp.float32)
        for j in range(rows.shape[0] // LANES):
            tile = rows[pl.ds(j * LANES, LANES), :]
            out[f, :, pl.ds(j * LANES, LANES)] = tile.T.astype(out.dtype)


def tuned(queries, keys, values, norm_gain, conv_weight):
    _, frames, pixels, width = queries.shape
    cols = conv_weight.shape[2]
    axes = ("groups", "strip")
    groups, devices = lax.axis_size("groups"), lax.axis_size("strip")
    strips = devices // TB
    x, s = lax.axis_index("groups"), lax.axis_index("strip")
    z, inside = s // strips, s % strips
    y, core = inside // 2, inside % 2

    def send(block, where):
        route = []
        for g in range(groups):
            for d in range(devices):
                to = where(g, d)
                if to is not None:
                    route.append((g * devices + d, to[0] * devices + to[1]))
        moved = lax.ppermute(block, axes, route)
        return vm(moved) if block.shape[1] == width else moved

    def to_core(g, d):
        return g, d ^ 1

    def to_y(g, d):
        return g, d ^ 2

    def to_x(g, d):
        return 1 - g, d

    def up(r):
        return lambda g, d: (g, d + r * strips) if d + r * strips < devices else None

    def along(**pairs):
        table = {int(a[1:]): b for a, b in pairs.items()}
        return lambda g, d: (
            (g, table[d // strips] * strips + d % strips) if d // strips in table else None
        )

    mine = inside.astype(jnp.int32).reshape(1)
    side = x.astype(jnp.int32).reshape(1)
    code = (x * devices // strips * 4 + z * 4 + y * 2 + core).astype(jnp.int32).reshape(1)
    k = keys[0].transpose(0, 2, 1)
    v = values[0].transpose(0, 2, 1)
    q = queries[0].transpose(0, 2, 1)
    q = vm(q)
    gain = vm(jnp.broadcast_to(norm_gain[:, None], (width, LANES)))

    rows = 3 * cols
    half = -(-rows // 16) * 8
    whole = conv_weight.transpose(0, 2, 1).reshape(rows, width)
    piece = half_of(side, whole, half, rows - half)
    rest = half_of(1 - side, whole, rows - half, half)
    zp1 = send(piece, along(z0=1, z1=0, z2=3, z3=2))
    zp2 = send(piece, along(z1=2, z2=1))
    zp3 = send(zp1, along(z1=2, z2=1))
    zp4 = send(zp2, along(z1=0, z2=3))
    zp5 = send(zp3, along(z1=0, z2=3))
    zr2 = send(rest, along(z1=2, z2=1))
    zr4 = send(zr2, along(z1=0, z2=3))
    outer = ((z == 0) | (z == TB - 1)).astype(jnp.int32).reshape(1)
    slot_b = pick(outer, zp4, zp2)
    rest_b = pick(outer, zr4, zr2)
    slot_c = pick(outer, zp5, zp3)
    y0 = send(piece, to_y)
    ya = send(zp1, to_y)
    yb = send(slot_b, to_y)
    yc = send(slot_c, to_y)
    early_pieces = [
        whole,
        y0,
        send(y0, to_x),
        zp1,
        send(zp1, to_x),
        ya,
        send(ya, to_x),
        slot_b,
        rest_b,
        slot_c,
        send(slot_c, to_x),
    ]
    late_pieces = [yb, send(rest_b, to_y), yc, send(yc, to_x)]

    quarter = width // 4
    kept, given = local_state(mine, k, v)
    from_core = send(given, to_core)
    chip = add_up(kept, from_core)
    from_y = send(chip[quarter:], to_y)
    plane = add_up(chip[:quarter], from_y)
    below = send(plane, up(1))
    two = add_up(plane, below)
    below = send(two, up(2))
    share = add_up(two, below)
    beside = send(share, to_y)
    states = [share, send(share, to_core), beside, send(beside, to_core)]
    states = [vm(s) for s in states]

    late = attend((1, 2), mine, q, states, gain)
    late_other = vm(send(late, to_core))
    early = attend((0,), mine, q, states, gain)
    early_other = vm(send(early, to_core))

    sums, rims = [], []
    for name, pieces in (("a", early_pieces), ("b", late_pieces)):
        count = cols * len(blocks_of("ab".index(name), z, y))
        rim, w = pl.pallas_call(
            functools.partial(rim_kernel, cols, "ab".index(name)),
            in_specs=[SMEM] + [VMEM] * (2 + len(pieces)),
            out_specs=[VMEM] * 2,
            out_shape=[
                pltpu.VMEM((count, 4 * pixels), jnp.bfloat16),
                pltpu.VMEM((3, count, width), jnp.bfloat16),
            ],
            compiler_params=limit(16),
            name="rim",
        )(code, late, late_other, *pieces)
        rim = send(rim, up(1))
        rims += [rim, send(rim, to_core)]
        keep, give = pl.pallas_call(
            own_kernel,
            in_specs=[VMEM] * 5,
            out_specs=[VMEM] * 2,
            out_shape=[pltpu.VMEM((count, 3 * pixels), jnp.float32)] * 2,
            compiler_params=limit(16),
            name="own",
        )(late, late_other, early, early_other, w)
        sums += [keep, vm(send(give, to_core))]

    result = pl.pallas_call(
        functools.partial(out_kernel, cols),
        in_specs=[SMEM] + [VMEM] * 8,
        out_specs=VMEM,
        out_shape=jax.ShapeDtypeStruct((frames, pixels, cols * devices), jnp.bfloat16),
        scratch_shapes=[pltpu.VMEM((cols * devices, pixels), jnp.float32)],
        compiler_params=limit(16),
        name="out",
    )(code, *sums, *[vm(rim) for rim in rims])
    return result[None]


def solution(mesh):
    placed = (
        P(("groups", "strip"), None, None, None),
        P(("groups", "strip"), None, None, None),
        P(("groups", "strip"), None, None, None),
        P(),
        P(None, None, "strip"),
    )

    groups, devices = mesh.shape["groups"], mesh.shape["strip"]
    square = groups == 2 and devices == 4 * TB

    def per_device(queries, keys, values, norm_gain, conv_weight):
        _, frames, pixels, width = queries.shape
        cols = conv_weight.shape[2]
        fits = (
            square
            and frames == 3
            and pixels == LANES
            and width == H * DH
            and cols % 8 == 0
            and cols * devices % LANES == 0
        )
        form = tuned if fits else generic
        return form(queries, keys, values, norm_gain, conv_weight)

    return jax.shard_map(
        per_device,
        mesh=mesh,
        in_specs=placed,
        out_specs=P(("groups", "strip"), None, None, None),
        check_vma=False,
    )
```
